256 devices in a mesh: group: 64 (over y, z, core), mp: 4 (over x).
Axes of the slice: x: 4, y: 4, z: 8, core: 2. Of those that a mesh axis runs over, the one named last changes fastest.
Arguments:
- database: bfloat16 [384, 128, 4096], P('group', 'mp'), may hold values from -6 to 6
- head_weight: bfloat16 [4096, 2048], P(None, 'mp'), may hold values from -0.09375 to 0.09375
- value_weight: bfloat16 [4096, 2048], P(None, 'mp'), may hold values from -0.09375 to 0.09375
- segment_query: bfloat16 [53248, 2048], P('group', 'mp'), may hold values from -90 to 90
- segment_key: bfloat16 [53248, 2048], P('group', 'mp'), may hold values from -90 to 90
- segment_value: bfloat16 [53248, 2048], P('group', 'mp'), may hold values from -6 to 6
- owner_shard: int32 [832, 2], P('group'), may hold values from 0 to 63, as said below
- entry_slot: int32 [832, 2], P('group'), may hold values from 0 to 5
Outputs:
- attended: bfloat16 [53248, 2048], P('group', 'mp')
The draws below stay inside these ranges and needn't reach their ends.
Inputs may be any that keep to these rules, and one draw needn't show every extreme that they name: `owner_shard`: among the rows of one index of group no shard is named more than 1 times, and one shard is named exactly 1 times by the rows of every index.
All inputs are finite; a program needn't handle non-finite values.
Results may differ from the reference program's by a relative error of at most 0.025.
The reference program's roundings to bfloat16 on the way count: a program that leaves them out, or rounds other values in their place, can miss the bound.
Values may be sent and summed in bfloat16 or wider, within the bound.
No kernel may reach another device: no remote copies, remote signals or barrier semaphores. Data moves between devices by JAX's collectives and lax.ppermute only.
A program may use at most 128 MiB of HBM per device.

```python
import jax
import jax.numpy as jnp
from jax import lax

D = 4096
HEADS = 16
HEAD_DIM = 128
SEG_LEN = 64
NBR_LEN = 128
NEIGH = 2
SEG_DEV = 13
NBR_DEV = 6
INNER = 2048
SEGMENTS = 832
TOKENS = 53248
NBRS = 384
CAP = 1


def shuffle_one(shuffle_key, picked_row):
    return jax.random.permutation(shuffle_key, picked_row)


def draw_owner_shard(key, part):
    owners = SEGMENTS // SEG_DEV
    database_size = owners * CAP
    requests = SEG_DEV * NEIGH
    key_base, key_level, key_hot, key_perm = jax.random.split(jax.random.fold_in(key, 11), 4)
    starting_score = jax.random.randint(key_base, (owners, database_size), 0, 4096)
    score_level = jax.random.randint(key_level, (owners,), 0, 5)
    busiest_entry = jax.random.randint(key_hot, (), 0, owners)
    database_owner = jnp.arange(database_size, dtype=jnp.int32) // CAP
    extra_reward = score_level[database_owner] * 4096 + jnp.where(database_owner == busiest_entry, 262144, 0)
    entry_score = (starting_score + extra_reward[None, :]) * database_size + jnp.arange(database_size, dtype=jnp.int32)[None, :]
    picked = lax.top_k(entry_score, requests)[1].astype(jnp.int32)
    shuffle_keys = jax.random.split(key_perm, owners)
    shuffled = jax.vmap(shuffle_one)(shuffle_keys, picked)
    return (shuffled // CAP).reshape(SEGMENTS, NEIGH).astype(jnp.int32)


def peaked_rows(key, shape):
    return jnp.clip(jax.random.normal(key, shape, jnp.float32), -6.0, 6.0)


def draw_segment_query(key, part):
    return peaked_rows(jax.random.fold_in(key, 21), (TOKENS, INNER)).astype(jnp.bfloat16)


def draw_segment_key(key, part):
    return peaked_rows(jax.random.fold_in(key, 31), (TOKENS, INNER)).astype(jnp.bfloat16)


def set_ends(array, stream_key, low, largest):
    place = [jax.random.randint(jax.random.fold_in(stream_key, axis), (), 0, length) for axis, length in enumerate(array.shape)]
    longest = array.shape.index(max(array.shape))
    neighbour = place[:longest] + [(place[longest] + 1) % array.shape[longest]] + place[longest + 1:]
    return array.at[tuple(place)].set(low).at[tuple(neighbour)].set(largest)


def level_of(rng, shape, cuts, least, largest):
    def one(position, parts):
        draws = jax.random.uniform(jax.random.fold_in(jax.random.fold_in(rng, 6), position), (parts,), jnp.float32, least / len(cuts), largest / len(cuts))
        return jnp.repeat(jnp.exp(draws), shape[position] // parts).reshape((-1,) + (1,) * (len(shape) - position - 1))

    loudness = one(*cuts[0])
    for cut in cuts[1:]:
        loudness = loudness * one(*cut)
    return loudness


def bell_draw(stream_key, extent, spread, limit, shards=(), kind=jnp.bfloat16):
    result = spread * jax.random.normal(stream_key, extent, jnp.float32)
    if shards:
        result = result * level_of(stream_key, extent, shards, -0.22, 0.18)
    return jnp.clip(result, -limit, limit).astype(kind)


def setup_inputs(seed: int = 0) -> dict:
    seeds = jax.random.split(jax.random.key(seed), 9)
    return {
        "database": bell_draw(seeds[0], (NBRS, NBR_LEN, D), 1.0, 6.0, ((0, 64), (1, 4))),
        "head_weight": bell_draw(seeds[1], (D, INNER), D ** -0.5, 0.09375, ((1, 4),)),
        "value_weight": bell_draw(seeds[2], (D, INNER), D ** -0.5, 0.09375, ((1, 4),)),
        "segment_query": draw_segment_query(jax.random.fold_in(seeds[8], 71), 0),
        "segment_key": draw_segment_key(jax.random.fold_in(seeds[8], 71), 0),
        "segment_value": bell_draw(seeds[5], (TOKENS, INNER), 1.0, 6.0, ((0, 64), (1, 4))),
        "owner_shard": draw_owner_shard(jax.random.fold_in(seeds[8], 71), 0),
        "entry_slot": set_ends(jax.random.randint(seeds[7], (SEGMENTS, NEIGH), 0, NBR_DEV), jax.random.fold_in(seeds[7], 1), 0, NBR_DEV - 1).astype(jnp.int32),
    }


def reference(database, head_weight, value_weight, segment_query, segment_key, segment_value, owner_shard, entry_slot):
    factor = HEAD_DIM ** -0.5

    def project_rows(rows_block):
        heads_part = jnp.dot(rows_block, head_weight, preferred_element_type=jnp.float32).astype(jnp.bfloat16)
        values_part = jnp.dot(rows_block, value_weight, preferred_element_type=jnp.float32).astype(jnp.bfloat16)
        return heads_part, values_part

    head_states, value_states = lax.map(project_rows, database)
    neighbour_pairs = (owner_shard * NBR_DEV + entry_slot).astype(jnp.int32)
    queries = segment_query.reshape(SEGMENTS, SEG_LEN, HEADS, HEAD_DIM)
    seg_keys = segment_key.reshape(SEGMENTS, SEG_LEN, HEADS, HEAD_DIM)
    seg_values = segment_value.reshape(SEGMENTS, SEG_LEN, HEADS, HEAD_DIM)

    def one_segment(operands):
        query_block, key_block, value_block, neighbour_pair = operands
        head_rows = head_states[neighbour_pair].reshape(NEIGH, NBR_LEN, HEADS, HEAD_DIM).astype(jnp.float32)
        value_matrix_rows = value_states[neighbour_pair].reshape(NEIGH * NBR_LEN, HEADS, HEAD_DIM).astype(jnp.float32)
        scores = jnp.einsum("jnhd,thd->jhnt", head_rows, key_block.astype(jnp.float32), precision=lax.Precision.HIGHEST) * factor
        weights = jax.nn.softmax(scores, axis=-1).astype(jnp.bfloat16)
        encoded = (head_rows + jnp.einsum("jhnt,thd->jnhd", weights.astype(jnp.float32), value_block.astype(jnp.float32), precision=lax.Precision.HIGHEST)).astype(jnp.bfloat16)
        cross = jnp.einsum("thd,jnhd->htjn", query_block.astype(jnp.float32), encoded.astype(jnp.float32), precision=lax.Precision.HIGHEST) * factor
        cross = cross.reshape(HEADS, SEG_LEN, NEIGH * NBR_LEN)
        blend_weights = jax.nn.softmax(cross, axis=-1)
        final_output = jnp.einsum("wgs,swy->gwy", blend_weights, value_matrix_rows, precision=lax.Precision.HIGHEST)
        return final_output.reshape(SEG_LEN, INNER).astype(jnp.bfloat16)

    outputs = lax.map(one_segment, (queries, seg_keys, seg_values, neighbour_pairs))
    return outputs.reshape(TOKENS, INNER)
```

```python
import functools

import jax
import jax.numpy as jnp
from jax import lax
from jax.experimental import pallas as pl
from jax.experimental.pallas import tpu as pltpu
from jax.sharding import Mesh
from jax.sharding import PartitionSpec as P

HEAD_DIM = 128
NY, NZ, NC = 4, 8, 2
PLANE = NY * NC
DELTAS = (0, 7, 1, 6, 2, 5, 3, 4)
NEAR = 5
STAT = 128


def project_kernel(n_parts, *refs):
    parts, (hw, vw, out, acc) = refs[:n_parts], refs[n_parts:]
    k = pl.program_id(0)
    entries = out.shape[0]
    width = hw.shape[1]

    @pl.when(k == 0)
    def _():
        acc[...] = jnp.zeros_like(acc)

    row = 0
    for part in parts:
        rows = part.shape[1]
        x = part[...].reshape(entries * rows, part.shape[2])
        span = pl.ds(row, entries * rows)
        acc[span, :width] += jnp.dot(x, hw[...], preferred_element_type=jnp.float32)
        acc[span, width:] += jnp.dot(x, vw[...], preferred_element_type=jnp.float32)
        row += entries * rows

    @pl.when(k == pl.num_programs(0) - 1)
    def _():
        row = 0
        at = 0
        for part in parts:
            rows = part.shape[1]
            block = acc[pl.ds(row, entries * rows), :].astype(out.dtype)
            out[:, at : at + rows, :] = block.reshape(entries, rows, 2 * width)
            row += entries * rows
            at += rows


def project(parts, head_weight, value_weight):
    entries, _, depth = parts[0].shape
    rows = sum(p.shape[1] for p in parts)
    width = head_weight.shape[1]
    step = 512
    return pl.pallas_call(
        functools.partial(project_kernel, len(parts)),
        grid=(depth // step,),
        in_specs=[
            pl.BlockSpec((entries, p.shape[1], step), lambda k: (0, 0, k)) for p in parts
        ]
        + [pl.BlockSpec((step, width), lambda k: (k, 0))] * 2,
        out_specs=pl.BlockSpec((entries, rows, 2 * width), lambda k: (0, 0, 0)),
        out_shape=jax.ShapeDtypeStruct((entries, rows, 2 * width), jnp.bfloat16),
        scratch_shapes=[pltpu.VMEM((entries * rows, 2 * width), jnp.float32)],
        compiler_params=pltpu.CompilerParams(vmem_limit_bytes=40 << 20),
        cost_estimate=pl.CostEstimate(
            flops=4 * entries * rows * depth * width,
            bytes_accessed=4 * depth * width + 2 * entries * rows * (depth + 2 * width),
            transcendentals=0,
        ),
        name="project",
    )(*parts, head_weight, value_weight)


def attend_kernel(n_pieces, slot, seg_at, entry_at, used_at, q, k, v, *refs):
    pieces, out = refs[:n_pieces], refs[-1]
    width = q.shape[2]
    factor = HEAD_DIM**-0.5

    @pl.when(used_at[slot * PLANE + pl.program_id(0)] != 0)
    def _():
        lanes = lax.broadcasted_iota(jnp.int32, (q.shape[1], STAT), 1)
        stats = jnp.zeros((q.shape[1], STAT), jnp.float32)
        for h in range(width // HEAD_DIM):
            cols = slice(h * HEAD_DIM, (h + 1) * HEAD_DIM)
            vcols = slice(width + h * HEAD_DIM, width + (h + 1) * HEAD_DIM)
            states = jnp.concatenate([p[0, :, cols] for p in pieces], axis=0)
            values = jnp.concatenate([p[0, :, vcols] for p in pieces], axis=0)
            scores = (
                lax.dot_general(
                    k[0, :, cols], states, (((1,), (1,)), ((), ())),
                    preferred_element_type=jnp.float32,
                )
                * factor
            )
            scores = jnp.exp(scores - jnp.max(scores, axis=0, keepdims=True))
            weights = (scores / jnp.sum(scores, axis=0, keepdims=True)).astype(jnp.bfloat16)
            encoded = (
                states.astype(jnp.float32)
                + lax.dot_general(
                    weights, v[0, :, cols], (((0,), (0,)), ((), ())),
                    preferred_element_type=jnp.float32,
                )
            ).astype(jnp.bfloat16)
            cross = (
                lax.dot_general(
                    q[0, :, cols], encoded, (((1,), (1,)), ((), ())),
                    preferred_element_type=jnp.float32,
                )
                * factor
            )
            highest = jnp.max(cross, axis=1, keepdims=True)
            mix = jnp.exp(cross - highest)
            total = jnp.sum(mix, axis=1, keepdims=True)
            upper = mix.astype(jnp.bfloat16)
            lower = (mix - upper.astype(jnp.float32)).astype(jnp.bfloat16)
            both = jnp.dot(
                jnp.concatenate([upper, lower], axis=0), values,
                preferred_element_type=jnp.float32,
            )
            share = both[: mix.shape[0]] + both[mix.shape[0] :]
            out[0, 0, :, cols] = (share / total).astype(out.dtype)
            rest = highest + jnp.log(total)
            for j in range(3):
                part = rest.astype(jnp.bfloat16).astype(jnp.float32)
                stats = jnp.where(lanes == 3 * h + j, part, stats)
                rest = rest - part
        out[0, 0, :, width:] = stats.astype(out.dtype)


def attend(slot, place, places, tables, q, k, v, pieces, buffer):
    segs, seg_len, width = q.shape
    seg_dev = segs // PLANE
    block = pl.BlockSpec(
        (1, seg_len, width),
        lambda g, seg, entry, used: (g * seg_dev + seg[slot * PLANE + g], 0, 0),
    )
    shape = jax.ShapeDtypeStruct((PLANE, places, seg_len, width + STAT), jnp.bfloat16)
    in_specs = [block] * 3 + [
        pl.BlockSpec(
            (1,) + p.shape[1:], lambda g, seg, entry, used: (entry[slot * PLANE + g], 0, 0)
        )
        for p in pieces
    ]
    args = [*tables, q, k, v, *pieces]
    aliases = {}
    if buffer is not None:
        aliases = {len(args): 0}
        args.append(buffer)
        in_specs.append(pl.BlockSpec(memory_space=pl.ANY))
    rows = sum(p.shape[1] for p in pieces)
    heads = width // HEAD_DIM
    return pl.pallas_call(
        functools.partial(attend_kernel, len(pieces), slot),
        grid_spec=pltpu.PrefetchScalarGridSpec(
            num_scalar_prefetch=3,
            grid=(PLANE,),
            in_specs=in_specs,
            out_specs=pl.BlockSpec(
                (1, 1, seg_len, width + STAT), lambda g, seg, entry, used: (g, place, 0, 0)
            ),
        ),
        out_shape=shape,
        input_output_aliases=aliases,
        compiler_params=pltpu.CompilerParams(vmem_limit_bytes=40 << 20),
        cost_estimate=pl.CostEstimate(
            flops=PLANE * heads * 10 * rows * seg_len * HEAD_DIM,
            bytes_accessed=PLANE * 2 * (4 * seg_len * width + 2 * rows * width),
            transcendentals=PLANE * heads * 2 * rows * seg_len,
        ),
        name="attend",
    )(*args)


def combine_kernel(src, far, slot, near0, far0, near1, far1, out):
    s = pl.program_id(0)
    width = out.shape[1]
    first = jnp.where(far[2 * s] != 0, far0[0, 0], near0[0, 0]).astype(jnp.float32)
    second = jnp.where(far[2 * s + 1] != 0, far1[0, 0], near1[0, 0]).astype(jnp.float32)
    for h in range(width // HEAD_DIM):
        cols = slice(h * HEAD_DIM, (h + 1) * HEAD_DIM)
        at = width + 3 * h
        one = first[:, at : at + 1] + first[:, at + 1 : at + 2] + first[:, at + 2 : at + 3]
        two = second[:, at : at + 1] + second[:, at + 1 : at + 2] + second[:, at + 2 : at + 3]
        peak = jnp.maximum(one, two)
        one = jnp.exp(one - peak)
        two = jnp.exp(two - peak)
        mixed = first[:, cols] * one + second[:, cols] * two
        out[:, cols] = (mixed / (one + two)).astype(out.dtype)


def combine(near, far, src, is_far, slot):
    seg_dev = src.shape[0] // 2
    _, _, seg_len, full = near.shape

    def pick(j, wants):
        def index(s, src, is_far, slot):
            here = is_far[2 * s + j] == wants
            return (
                jnp.where(here, src[2 * s + j], 0),
                jnp.where(here, slot[2 * s + j], 0),
                0,
                0,
            )

        return pl.BlockSpec((1, 1, seg_len, full), index)

    return pl.pallas_call(
        combine_kernel,
        grid_spec=pltpu.PrefetchScalarGridSpec(
            num_scalar_prefetch=3,
            grid=(seg_dev,),
            in_specs=[pick(0, 0), pick(0, 1), pick(1, 0), pick(1, 1)],
            out_specs=pl.BlockSpec((seg_len, full - STAT), lambda s, a, b, c: (s, 0)),
        ),
        out_shape=jax.ShapeDtypeStruct((seg_dev * seg_len, full - STAT), jnp.bfloat16),
        name="combine",
    )(src, is_far, slot, near, far, near, far)


def hop(x, axis, step):
    n = lax.axis_size(axis)
    return lax.ppermute(x, axis, [(i, (i + step) % n) for i in range(n)])


def per_device(
    database,
    head_weight,
    value_weight,
    segment_query,
    segment_key,
    segment_value,
    owner_shard,
    entry_slot,
):
    entries, rows, _ = database.shape
    seg_dev = owner_shard.shape[0]
    seg_len = segment_query.shape[0] // seg_dev
    width = segment_query.shape[1]
    y, z, c = lax.axis_index("y"), lax.axis_index("z"), lax.axis_index("c")

    wanted = (owner_shard * entries + entry_slot).reshape(-1).astype(jnp.int32)
    plane_wanted = lax.all_gather(wanted, ("y", "c"), axis=0, tiled=False)
    deltas = jnp.array(DELTAS, jnp.int32)
    shards = (y * NZ + (z + deltas) % NZ) * NC + c
    match = (plane_wanted // entries)[None] == shards[:, None, None]
    asks = jnp.arange(wanted.shape[0], dtype=jnp.int32)
    used = jnp.any(match, axis=2).astype(jnp.int32).reshape(-1)
    seg_at = jnp.sum(jnp.where(match, asks // 2, 0), axis=2).reshape(-1)
    entry_at = jnp.sum(jnp.where(match, (plane_wanted % entries)[None], 0), axis=2).reshape(-1)
    tables = (seg_at, entry_at, used)

    from_left, from_right = hop(database, "mp", 1), hop(database, "mp", -1)
    half = rows // 2
    far_a = hop(from_left[:, :half], "mp", 1)
    far_b = hop(from_right[:, half:], "mp", -1)
    own = [
        project([database], head_weight, value_weight),
        project([from_left, from_right], head_weight, value_weight),
        project([far_a, far_b], head_weight, value_weight),
    ]
    held = [own]
    forward = backward = own
    for _ in range(NZ // 2 - 1):
        forward = [hop(p, "z", 1) for p in forward]
        backward = [hop(p, "z", -1) for p in backward]
        held += [forward, backward]
    last = []
    for f, b in zip(forward, backward):
        cut = f.shape[1] // 2
        last += [hop(f[:, :cut], "z", 1), hop(b[:, cut:], "z", -1)]
    held.append(last)

    keys = lax.all_gather(segment_key, ("y", "c"), axis=0, tiled=True)
    values = lax.all_gather(segment_value, ("y", "c"), axis=0, tiled=True)
    queries = lax.all_gather(segment_query, ("y", "c"), axis=0, tiled=True)
    keys, values, queries = (a.reshape(-1, seg_len, width) for a in (keys, values, queries))

    back = []
    for begin, end in ((0, NEAR), (NEAR, NZ)):
        buffer = None
        for slot in range(begin, end):
            buffer = attend(
                slot, slot - begin, end - begin, tables, queries, keys, values, held[slot], buffer
            )
        back.append(lax.all_to_all(buffer, ("y", "c"), split_axis=0, concat_axis=0, tiled=True))

    owner = owner_shard.reshape(-1)
    delta = (owner // NC % NZ - z) % NZ
    slot = jnp.where(delta < NZ // 2, 2 * delta, 2 * (NZ - delta) - 1)
    src = owner // (NC * NZ) * NC + owner % NC
    is_far = (slot >= NEAR).astype(jnp.int32)
    return combine(back[0], back[1], src, is_far, jnp.where(slot >= NEAR, slot - NEAR, slot))


def solution(mesh):
    grid = Mesh(mesh.devices.reshape(NY, NZ, NC, -1), ("y", "z", "c", "mp"))
    group = ("y", "z", "c")
    in_specs = (
        P(group, "mp", None),
        P(None, "mp"),
        P(None, "mp"),
        P(group, "mp"),
        P(group, "mp"),
        P(group, "mp"),
        P(group, None),
        P(group, None),
    )
    return jax.shard_map(
        per_device, mesh=grid, in_specs=in_specs, out_specs=P(group, "mp"), check_vma=False
    )
```

```python
import functools

import jax
import jax.numpy as jnp
from jax import lax
from jax.experimental import pallas as pl
from jax.experimental.pallas import tpu as pltpu
from jax.sharding import Mesh
from jax.sharding import PartitionSpec as P

HEAD_DIM = 128
NY, NZ, NC = 4, 8, 2
PLANE = NY * NC
DELTAS = (0, 7, 1, 6, 2, 5, 3, 4)
CHUNKS = ((0, 1, 2), (3, 4), (5, 6), (7,))
STAT = 128
LANES = 16
PAIR = 2


def project_kernel(parts, hw, vw, out, *scratch):
    rows_in, hbuf, vbuf, acc, in_sem, sem = (scratch[:-5], *scratch[-5:])
    entries, _, width = out.shape
    width //= 2
    steps, depth, _ = hbuf.shape
    loads = [pltpu.make_async_copy(p, r, in_sem.at[i]) for i, (p, r) in enumerate(zip(parts, rows_in))]
    weights = [
        [
            pltpu.make_async_copy(w.at[pl.ds(k * depth, depth)], buf.at[k], sem.at[i, k])
            for i, (w, buf) in enumerate(((hw, hbuf), (vw, vbuf)))
        ]
        for k in range(steps)
    ]
    for copy in loads:
        copy.start()
    for pair in weights:
        for copy in pair:
            copy.start()
    for copy in loads:
        copy.wait()
    for k in range(steps):
        for copy in weights[k]:
            copy.wait()
        row = 0
        for r in rows_in:
            count = entries * r.shape[1]
            x = r[:, :, k * depth : (k + 1) * depth].reshape(count, depth)
            for side, buf in ((0, hbuf), (1, vbuf)):
                span = (slice(row, row + count), slice(side * width, (side + 1) * width))
                y = jnp.dot(x, buf[k], preferred_element_type=jnp.float32)
                acc[span] = y if k == 0 else acc[span] + y
            row += count
    row = at = 0
    for r in rows_in:
        rows = r.shape[1]
        block = acc[row : row + entries * rows, :].astype(out.dtype)
        out[:, at : at + rows, :] = block.reshape(entries, rows, 2 * width)
        row += entries * rows
        at += rows


def project(parts, head_weight, value_weight):
    entries, _, depth = parts[0].shape
    rows = sum(p.shape[1] for p in parts)
    width = head_weight.shape[1]
    steps = 8
    n = len(parts)

    def kernel(*refs):
        project_kernel(refs[:n], *refs[n:])

    chunk = pltpu.VMEM((steps, depth // steps, width), jnp.bfloat16)
    return pl.pallas_call(
        kernel,
        in_specs=[pl.BlockSpec(memory_space=pl.ANY)] * (n + 2),
        out_specs=pl.BlockSpec(memory_space=pltpu.VMEM),
        out_shape=jax.ShapeDtypeStruct((entries, rows, 2 * width), jnp.bfloat16),
        scratch_shapes=[pltpu.VMEM(p.shape, p.dtype) for p in parts]
        + [
            chunk,
            chunk,
            pltpu.VMEM((entries * rows, 2 * width), jnp.float32),
            pltpu.SemaphoreType.DMA((n,)),
            pltpu.SemaphoreType.DMA((2, steps)),
        ],
        compiler_params=pltpu.CompilerParams(vmem_limit_bytes=60 << 20),
        cost_estimate=pl.CostEstimate(
            flops=4 * entries * rows * depth * width,
            bytes_accessed=4 * depth * width + 2 * entries * rows * (depth + 2 * width),
            transcendentals=0,
        ),
        name="project",
    )(*parts, head_weight, value_weight)


def matmul(a, b, da, db):
    return lax.dot_general(
        a, b, (((da,), (db,)), ((), ())), preferred_element_type=jnp.float32
    )


def attend_kernel(slots, counts, seg_at, entry_at, used_at, *refs):
    refs = list(refs)
    out = refs.pop()
    qkvs = [[refs.pop(0) for _ in range(PAIR)] for _ in slots]
    held = [[[refs.pop(0) for _ in range(PAIR)] for _ in range(n)] for n in counts]
    seg_len, width = out.shape[1], qkvs[0][0].shape[2] // 3
    factor = HEAD_DIM**-0.5
    lanes = lax.broadcasted_iota(jnp.int32, (seg_len, STAT), 1)
    units = [(s, h) for s in range(PAIR) for h in range(width // HEAD_DIM)]

    def part(ref, index, h):
        begin = index * width + h * HEAD_DIM
        return ref[0, :, begin : begin + HEAD_DIM]

    def run(place, qkv, pieces):
        def rows_of(s, index, h):
            return jnp.concatenate([part(p[s], index, h) for p in pieces], axis=0)

        states = [rows_of(s, 0, h) for s, h in units]
        scores = [
            matmul(part(qkv[s], 1, h), x, 1, 1) * factor for (s, h), x in zip(units, states)
        ]
        peaks = [jnp.max(x, axis=0, keepdims=True) for x in scores]
        scores = [jnp.exp(x - m) for x, m in zip(scores, peaks)]
        weights = [
            (x * (1.0 / jnp.sum(x, axis=0, keepdims=True))).astype(jnp.bfloat16) for x in scores
        ]
        encoded = [
            (x.astype(jnp.float32) + matmul(w, part(qkv[s], 2, h), 0, 0)).astype(jnp.bfloat16)
            for (s, h), x, w in zip(units, states, weights)
        ]
        cross = [
            matmul(part(qkv[s], 0, h), x, 1, 1) * factor for (s, h), x in zip(units, encoded)
        ]
        highest = [jnp.max(x, axis=1, keepdims=True) for x in cross]
        mix = [jnp.exp(x - m) for x, m in zip(cross, highest)]
        totals = [jnp.sum(x, axis=1, keepdims=True) for x in mix]
        shares = []
        for (s, h), x in zip(units, mix):
            upper = x.astype(jnp.bfloat16)
            lower = (x - upper.astype(jnp.float32)).astype(jnp.bfloat16)
            both = matmul(jnp.concatenate([upper, lower], axis=0), rows_of(s, 1, h), 1, 0)
            shares.append(both[:seg_len] + both[seg_len:])
        stats = [out[s, :, len(slots) * width :].astype(jnp.float32) for s in range(PAIR)]
        for (s, h), share, total, high in zip(units, shares, totals, highest):
            begin = place * width + h * HEAD_DIM
            out[s, :, begin : begin + HEAD_DIM] = (share * (1.0 / total)).astype(out.dtype)
            rest = high + jnp.log(total)
            for j in range(3):
                term = rest.astype(jnp.bfloat16).astype(jnp.float32)
                stats[s] = jnp.where(lanes == place * LANES + 3 * h + j, term, stats[s])
                rest = rest - term
        for s in range(PAIR):
            out[s, :, len(slots) * width :] = stats[s].astype(out.dtype)

    for place, (slot, qkv, pieces) in enumerate(zip(slots, qkvs, held)):
        at = slot * PLANE + pl.program_id(0) * PAIR
        used = used_at[at]
        for s in range(1, PAIR):
            used = used | used_at[at + s]
        pl.when(used != 0)(functools.partial(run, place, qkv, pieces))


def attend(slots, tables, qkv, held):
    segs, seg_len, width = qkv.shape
    width //= 3
    seg_dev = segs // PLANE

    def seg_spec(slot, s):
        def index(i, seg, entry, used):
            g = i * PAIR + s
            return g * seg_dev + seg[slot * PLANE + g], 0, 0

        return pl.BlockSpec((1, seg_len, 3 * width), index)

    def piece_spec(piece, slot, s):
        return pl.BlockSpec(
            (1,) + piece.shape[1:],
            lambda i, seg, entry, used: (entry[slot * PLANE + i * PAIR + s], 0, 0),
        )

    in_specs = [seg_spec(slot, s) for slot in slots for s in range(PAIR)]
    args = [*tables] + [qkv] * len(in_specs)
    for slot in slots:
        for piece in held[slot]:
            in_specs += [piece_spec(piece, slot, s) for s in range(PAIR)]
            args += [piece] * PAIR
    full = len(slots) * width + STAT
    return pl.pallas_call(
        functools.partial(attend_kernel, slots, [len(held[slot]) for slot in slots]),
        grid_spec=pltpu.PrefetchScalarGridSpec(
            num_scalar_prefetch=3,
            grid=(PLANE // PAIR,),
            in_specs=in_specs,
            out_specs=pl.BlockSpec((PAIR, seg_len, full), lambda i, *_: (i, 0, 0)),
        ),
        out_shape=jax.ShapeDtypeStruct((PLANE, seg_len, full), jnp.bfloat16),
        compiler_params=pltpu.CompilerParams(vmem_limit_bytes=60 << 20),
        cost_estimate=pl.CostEstimate(flops=1 << 20, bytes_accessed=1 << 20, transcendentals=0),
        name="attend",
    )(*args)


def combine_kernel(src, slot, *refs):
    backs, out = refs[:-1], refs[-1]
    seg_len = backs[0].shape[1]
    width = out.shape[1]

    def part(i, begin, size, per_place):
        value = None
        for slots, back in zip(CHUNKS, backs):
            here = (slot[i] >= slots[0]) & (slot[i] <= slots[-1])
            offset = jnp.where(here, slot[i] - slots[0], 0) * per_place + begin(len(slots))
            block = back[src[i], :, pl.ds(pl.multiple_of(offset, 128), size)]
            value = block if value is None else jnp.where(here, block, value)
        return value.astype(jnp.float32)

    def total(i):
        first = 0
        for slots in CHUNKS:
            here = (slot[i] >= slots[0]) & (slot[i] <= slots[-1])
            first = jnp.where(here, (slot[i] - slots[0]) * LANES, first)
        x = part(i, lambda n: n * width, STAT, 0)
        x = pltpu.roll(x, STAT - first, 1)
        return x + pltpu.roll(x, STAT - 1, 1) + pltpu.roll(x, STAT - 2, 1)

    @pl.loop(0, out.shape[0] // seg_len)
    def _(s):
        more = total(2 * s + 1) - total(2 * s)
        one = 1.0 / (1.0 + jnp.exp(more))
        two = 1.0 / (1.0 + jnp.exp(-more))
        rows = pl.ds(pl.multiple_of(s * seg_len, seg_len), seg_len)
        for h in range(width // HEAD_DIM):
            first = part(2 * s, lambda n: h * HEAD_DIM, HEAD_DIM, width)
            second = part(2 * s + 1, lambda n: h * HEAD_DIM, HEAD_DIM, width)
            lane = slice(3 * h, 3 * h + 1)
            out[rows, h * HEAD_DIM : (h + 1) * HEAD_DIM] = (
                first * one[:, lane] + second * two[:, lane]
            ).astype(out.dtype)


def combine(backs, src, slot):
    _, seg_len, full = backs[0].shape
    width = (full - STAT) // len(CHUNKS[0])
    return pl.pallas_call(
        combine_kernel,
        in_specs=[pl.BlockSpec(memory_space=pltpu.SMEM)] * 2
        + [pl.BlockSpec(memory_space=pltpu.VMEM)] * len(backs),
        out_specs=pl.BlockSpec(memory_space=pltpu.VMEM),
        out_shape=jax.ShapeDtypeStruct((src.shape[0] // 2 * seg_len, width), jnp.bfloat16),
        compiler_params=pltpu.CompilerParams(vmem_limit_bytes=60 << 20),
        name="combine",
    )(src, slot, *backs)


def hop(x, axis, step):
    n = lax.axis_size(axis)
    return lax.ppermute(x, axis, [(i, (i + step) % n) for i in range(n)])


def after(value, event):
    return lax.optimization_barrier((value, event))[0]


def ring(pieces, hops=NZ // 2):
    held = pieces if isinstance(pieces, list) else [[pieces]]
    while len(held) < min(2 * hops + 1, NZ):
        if len(held) < NZ - 1:
            forward, backward = held[-2:] if len(held) > 1 else held * 2
            held = held + [[hop(forward[0], "z", 1)], [hop(backward[0], "z", -1)]]
        else:
            (forward,), (backward,) = held[-2:]
            cut = forward.shape[1] // 2
            held = held + [[hop(forward[:, :cut], "z", 1), hop(backward[:, cut:], "z", -1)]]
    return held


def per_device(
    database,
    head_weight,
    value_weight,
    segment_query,
    segment_key,
    segment_value,
    owner_shard,
    entry_slot,
):
    entries, rows, _ = database.shape
    seg_dev = owner_shard.shape[0]
    seg_len = segment_query.shape[0] // seg_dev
    width = segment_query.shape[1]
    y, z, c = lax.axis_index("y"), lax.axis_index("z"), lax.axis_index("c")

    qkv = jnp.concatenate([segment_query, segment_key, segment_value], axis=1)
    qkv = lax.all_gather(qkv, ("y", "c"), axis=0, tiled=True).reshape(-1, seg_len, 3 * width)

    from_left, from_right = hop(database, "mp", 1), hop(database, "mp", -1)
    own = ring(project([database], head_weight, value_weight), 2)
    own[3:5], from_left, from_right = lax.optimization_barrier((own[3:5], from_left, from_right))
    half = rows // 2
    far_a = hop(from_left[:, :half], "mp", 1)
    far_b = hop(from_right[:, half:], "mp", -1)
    own = ring(own, 3)
    sides = project([from_left, from_right], head_weight, value_weight)
    sides, own[5:7], far_a, far_b = lax.optimization_barrier((sides, own[5:7], far_a, far_b))
    sides, own = ring(sides, 1), ring(own)
    far = [[project([far_a, far_b], head_weight, value_weight)]]
    sides[1:3], far = lax.optimization_barrier((sides[1:3], far))
    sides, far = ring(sides, 2), ring(far, 1)
    wanted = after((owner_shard * entries + entry_slot).reshape(-1), sides[1:3])
    plane_wanted = lax.all_gather(wanted, ("y", "c"), axis=0, tiled=False)
    sides[3:5], far[1:3], own[7], plane_wanted = lax.optimization_barrier(
        (sides[3:5], far[1:3], own[7], plane_wanted)
    )
    sides, far = ring(sides, 3), ring(far, 2)
    sides[5:7], far[3:5] = lax.optimization_barrier((sides[5:7], far[3:5]))

    deltas = jnp.array(DELTAS, jnp.int32)
    shards = (y * NZ + (z + deltas) % NZ) * NC + c
    match = (plane_wanted // entries)[None] == shards[:, None, None]
    asks = jnp.arange(wanted.shape[0], dtype=jnp.int32)
    used = jnp.any(match, axis=2).astype(jnp.int32).reshape(-1)
    seg_at = jnp.sum(jnp.where(match, asks // 2, 0), axis=2).reshape(-1)
    entry_at = jnp.sum(jnp.where(match, (plane_wanted % entries)[None], 0), axis=2).reshape(-1)
    tables = (seg_at, entry_at, used)

    def served(number):
        return attend(CHUNKS[number], tables, qkv, [sum(p, []) for p in zip(own, sides, far)])

    def back(share):
        return lax.all_to_all(share, ("y", "c"), split_axis=0, concat_axis=0, tiled=True)

    first = served(0)
    sides, far = ring(sides, 4), ring(far, 3)
    backs = [back(first)]
    tables = after(tables, first)
    second = served(1)
    sides[7], far[5:7], second = lax.optimization_barrier((sides[7], far[5:7], second))
    far = ring(far, 4)
    backs.append(back(after(second, backs[0])))
    tables = after(tables, backs[0])
    backs.append(back(after(served(2), backs[1])))
    backs.append(back(after(served(3), backs[2])))

    owner = owner_shard.reshape(-1)
    delta = (owner // NC % NZ - z) % NZ
    slot = jnp.where(delta < NZ // 2, 2 * delta, 2 * (NZ - delta) - 1)
    src = owner // (NC * NZ) * NC + owner % NC
    return combine(backs, src, slot)


def solution(mesh):
    grid = Mesh(mesh.devices.reshape(NY, NZ, NC, -1), ("y", "z", "c", "mp"))
    group = ("y", "z", "c")
    in_specs = (
        P(group, "mp", None),
        P(None, "mp"),
        P(None, "mp"),
        P(group, "mp"),
        P(group, "mp"),
        P(group, "mp"),
        P(group, None),
        P(group, None),
    )
    return jax.shard_map(
        per_device, mesh=grid, in_specs=in_specs, out_specs=P(group, "mp"), check_vma=False
    )
```

```python
import functools

import jax
import jax.numpy as jnp
from jax import lax
from jax.experimental import pallas as pl
from jax.experimental.pallas import tpu as pltpu
from jax.sharding import Mesh
from jax.sharding import PartitionSpec as P

HEAD_DIM = 128
NY, NZ, NC = 4, 8, 2
PLANE = NY * NC
DELTAS = (0, 7, 1, 6, 2, 5, 3, 4)
CHUNKS = ((0, 1, 2), (3, 4), (5, 6), (7,))
STAT = 128
LANES = 16
PAIR = 2


def project_kernel(parts, hw, vw, out, *scratch):
    rows_in, hbuf, vbuf, acc, in_sem, sem = (scratch[:-5], *scratch[-5:])
    entries, _, width = out.shape
    width //= 2
    steps, depth, _ = hbuf.shape
    loads = [pltpu.make_async_copy(p, r, in_sem.at[i]) for i, (p, r) in enumerate(zip(parts, rows_in))]
    weights = [
        [
            pltpu.make_async_copy(w.at[pl.ds(k * depth, depth)], buf.at[k], sem.at[i, k])
            for i, (w, buf) in enumerate(((hw, hbuf), (vw, vbuf)))
        ]
        for k in range(steps)
    ]
    for copy in loads:
        copy.start()
    for pair in weights:
        for copy in pair:
            copy.start()
    for copy in loads:
        copy.wait()
    for k in range(steps):
        for copy in weights[k]:
            copy.wait()
        row = 0
        for r in rows_in:
            count = entries * r.shape[1]
            x = r[:, :, k * depth : (k + 1) * depth].reshape(count, depth)
            for side, buf in ((0, hbuf), (1, vbuf)):
                span = (slice(row, row + count), slice(side * width, (side + 1) * width))
                y = jnp.dot(x, buf[k], preferred_element_type=jnp.float32)
                acc[span] = y if k == 0 else acc[span] + y
            row += count
    row = at = 0
    for r in rows_in:
        rows = r.shape[1]
        block = acc[row : row + entries * rows, :].astype(out.dtype)
        out[:, at : at + rows, :] = block.reshape(entries, rows, 2 * width)
        row += entries * rows
        at += rows


def project(parts, head_weight, value_weight):
    entries, _, depth = parts[0].shape
    rows = sum(p.shape[1] for p in parts)
    width = head_weight.shape[1]
    steps = 8
    n = len(parts)

    def kernel(*refs):
        project_kernel(refs[:n], *refs[n:])

    chunk = pltpu.VMEM((steps, depth // steps, width), jnp.bfloat16)
    return pl.pallas_call(
        kernel,
        in_specs=[pl.BlockSpec(memory_space=pl.ANY)] * (n + 2),
        out_specs=pl.BlockSpec(memory_space=pltpu.VMEM),
        out_shape=jax.ShapeDtypeStruct((entries, rows, 2 * width), jnp.bfloat16),
        scratch_shapes=[pltpu.VMEM(p.shape, p.dtype) for p in parts]
        + [
            chunk,
            chunk,
            pltpu.VMEM((entries * rows, 2 * width), jnp.float32),
            pltpu.SemaphoreType.DMA((n,)),
            pltpu.SemaphoreType.DMA((2, steps)),
        ],
        compiler_params=pltpu.CompilerParams(vmem_limit_bytes=60 << 20),
        cost_estimate=pl.CostEstimate(
            flops=4 * entries * rows * depth * width,
            bytes_accessed=4 * depth * width + 2 * entries * rows * (depth + 2 * width),
            transcendentals=0,
        ),
        name="project",
    )(*parts, head_weight, value_weight)


def matmul(a, b, da, db):
    return lax.dot_general(
        a, b, (((da,), (db,)), ((), ())), preferred_element_type=jnp.float32
    )


def attend_kernel(slots, counts, seg_at, entry_at, used_at, *refs):
    refs = list(refs)
    out = refs.pop()
    qkvs = [[refs.pop(0) for _ in range(PAIR)] for _ in slots]
    held = [[[refs.pop(0) for _ in range(PAIR)] for _ in range(n)] for n in counts]
    seg_len, width = out.shape[1], qkvs[0][0].shape[2] // 3
    factor = HEAD_DIM**-0.5
    lanes = lax.broadcasted_iota(jnp.int32, (seg_len, STAT), 1)
    units = [(s, h) for s in range(PAIR) for h in range(width // HEAD_DIM)]

    def part(ref, index, h):
        begin = index * width + h * HEAD_DIM
        return ref[0, :, begin : begin + HEAD_DIM]

    def run(place, qkv, pieces):
        def rows_of(s, index, h):
            return jnp.concatenate([part(p[s], index, h) for p in pieces], axis=0)

        states = [rows_of(s, 0, h) for s, h in units]
        scores = [
            matmul(part(qkv[s], 1, h), x, 1, 1) * factor for (s, h), x in zip(units, states)
        ]
        peaks = [jnp.max(x, axis=0, keepdims=True) for x in scores]
        scores = [jnp.exp(x - m) for x, m in zip(scores, peaks)]
        weights = [
            (x * (1.0 / jnp.sum(x, axis=0, keepdims=True))).astype(jnp.bfloat16) for x in scores
        ]
        encoded = [
            (x.astype(jnp.float32) + matmul(w, part(qkv[s], 2, h), 0, 0)).astype(jnp.bfloat16)
            for (s, h), x, w in zip(units, states, weights)
        ]
        cross = [
            matmul(part(qkv[s], 0, h), x, 1, 1) * factor for (s, h), x in zip(units, encoded)
        ]
        highest = [jnp.max(x, axis=1, keepdims=True) for x in cross]
        mix = [jnp.exp(x - m) for x, m in zip(cross, highest)]
        totals = [jnp.sum(x, axis=1, keepdims=True) for x in mix]
        shares = []
        for (s, h), x in zip(units, mix):
            upper = x.astype(jnp.bfloat16)
            lower = (x - upper.astype(jnp.float32)).astype(jnp.bfloat16)
            both = matmul(jnp.concatenate([upper, lower], axis=0), rows_of(s, 1, h), 1, 0)
            shares.append(both[:seg_len] + both[seg_len:])
        stats = [out[s, :, len(slots) * width :].astype(jnp.float32) for s in range(PAIR)]
        for (s, h), share, total, high in zip(units, shares, totals, highest):
            begin = place * width + h * HEAD_DIM
            out[s, :, begin : begin + HEAD_DIM] = (share * (1.0 / total)).astype(out.dtype)
            rest = high + jnp.log(total)
            for j in range(3):
                term = rest.astype(jnp.bfloat16).astype(jnp.float32)
                stats[s] = jnp.where(lanes == place * LANES + 3 * h + j, term, stats[s])
                rest = rest - term
        for s in range(PAIR):
            out[s, :, len(slots) * width :] = stats[s].astype(out.dtype)

    for place, (slot, qkv, pieces) in enumerate(zip(slots, qkvs, held)):
        at = slot * PLANE + pl.program_id(0) * PAIR
        used = used_at[at]
        for s in range(1, PAIR):
            used = used | used_at[at + s]
        pl.when(used != 0)(functools.partial(run, place, qkv, pieces))


def attend(slots, tables, qkv, held):
    segs, seg_len, width = qkv.shape
    width //= 3
    seg_dev = segs // PLANE

    def seg_spec(slot, s):
        def index(i, seg, entry, used):
            g = i * PAIR + s
            return g * seg_dev + seg[slot * PLANE + g], 0, 0

        return pl.BlockSpec((1, seg_len, 3 * width), index)

    def piece_spec(piece, slot, s):
        return pl.BlockSpec(
            (1,) + piece.shape[1:],
            lambda i, seg, entry, used: (entry[slot * PLANE + i * PAIR + s], 0, 0),
        )

    in_specs = [seg_spec(slot, s) for slot in slots for s in range(PAIR)]
    args = [*tables] + [qkv] * len(in_specs)
    for slot in slots:
        for piece in held[slot]:
            in_specs += [piece_spec(piece, slot, s) for s in range(PAIR)]
            args += [piece] * PAIR
    full = len(slots) * width + STAT
    return pl.pallas_call(
        functools.partial(attend_kernel, slots, [len(held[slot]) for slot in slots]),
        grid_spec=pltpu.PrefetchScalarGridSpec(
            num_scalar_prefetch=3,
            grid=(PLANE // PAIR,),
            in_specs=in_specs,
            out_specs=pl.BlockSpec((PAIR, seg_len, full), lambda i, *_: (i, 0, 0)),
        ),
        out_shape=jax.ShapeDtypeStruct((PLANE, seg_len, full), jnp.bfloat16),
        compiler_params=pltpu.CompilerParams(vmem_limit_bytes=60 << 20),
        cost_estimate=pl.CostEstimate(flops=len(slots) * (6 << 30), bytes_accessed=1 << 20, transcendentals=0),
        name="attend",
    )(*args)


def combine_kernel(src, slot, *refs):
    backs, out = refs[:-1], refs[-1]
    seg_len = backs[0].shape[1]
    width = out.shape[1]

    def part(i, begin, size, per_place):
        value = None
        for slots, back in zip(CHUNKS, backs):
            here = (slot[i] >= slots[0]) & (slot[i] <= slots[-1])
            offset = jnp.where(here, slot[i] - slots[0], 0) * per_place + begin(len(slots))
            block = back[src[i], :, pl.ds(pl.multiple_of(offset, 128), size)]
            value = block if value is None else jnp.where(here, block, value)
        return value.astype(jnp.float32)

    def total(i):
        first = 0
        for slots in CHUNKS:
            here = (slot[i] >= slots[0]) & (slot[i] <= slots[-1])
            first = jnp.where(here, (slot[i] - slots[0]) * LANES, first)
        x = part(i, lambda n: n * width, STAT, 0)
        x = pltpu.roll(x, STAT - first, 1)
        return x + pltpu.roll(x, STAT - 1, 1) + pltpu.roll(x, STAT - 2, 1)

    @pl.loop(0, out.shape[0] // seg_len)
    def _(s):
        more = total(2 * s + 1) - total(2 * s)
        one = 1.0 / (1.0 + jnp.exp(more))
        two = 1.0 / (1.0 + jnp.exp(-more))
        rows = pl.ds(pl.multiple_of(s * seg_len, seg_len), seg_len)
        for h in range(width // HEAD_DIM):
            first = part(2 * s, lambda n: h * HEAD_DIM, HEAD_DIM, width)
            second = part(2 * s + 1, lambda n: h * HEAD_DIM, HEAD_DIM, width)
            lane = slice(3 * h, 3 * h + 1)
            out[rows, h * HEAD_DIM : (h + 1) * HEAD_DIM] = (
                first * one[:, lane] + second * two[:, lane]
            ).astype(out.dtype)


def combine(backs, src, slot):
    _, seg_len, full = backs[0].shape
    width = (full - STAT) // len(CHUNKS[0])
    return pl.pallas_call(
        combine_kernel,
        in_specs=[pl.BlockSpec(memory_space=pltpu.SMEM)] * 2
        + [pl.BlockSpec(memory_space=pltpu.VMEM)] * len(backs),
        out_specs=pl.BlockSpec(memory_space=pltpu.VMEM),
        out_shape=jax.ShapeDtypeStruct((src.shape[0] // 2 * seg_len, width), jnp.bfloat16),
        compiler_params=pltpu.CompilerParams(vmem_limit_bytes=60 << 20),
        name="combine",
    )(src, slot, *backs)


def hop(x, axis, step):
    n = lax.axis_size(axis)
    return lax.ppermute(x, axis, [(i, (i + step) % n) for i in range(n)])


def after(value, event):
    return lax.optimization_barrier((value, event))[0]


def ring(pieces, hops=NZ // 2):
    held = pieces if isinstance(pieces, list) else [[pieces]]
    while len(held) < min(2 * hops + 1, NZ):
        if len(held) < NZ - 1:
            forward, backward = held[-2:] if len(held) > 1 else held * 2
            held = held + [[hop(forward[0], "z", 1)], [hop(backward[0], "z", -1)]]
        else:
            (forward,), (backward,) = held[-2:]
            cut = forward.shape[1] // 2
            held = held + [[hop(forward[:, :cut], "z", 1), hop(backward[:, cut:], "z", -1)]]
    return held


def per_device(
    database,
    head_weight,
    value_weight,
    segment_query,
    segment_key,
    segment_value,
    owner_shard,
    entry_slot,
):
    entries, rows, _ = database.shape
    seg_dev = owner_shard.shape[0]
    seg_len = segment_query.shape[0] // seg_dev
    width = segment_query.shape[1]
    y, z, c = lax.axis_index("y"), lax.axis_index("z"), lax.axis_index("c")

    qkv = jnp.concatenate([segment_query, segment_key, segment_value], axis=1)
    qkv = lax.all_gather(qkv, ("y", "c"), axis=0, tiled=True).reshape(-1, seg_len, 3 * width)

    from_left, from_right = hop(database, "mp", 1), hop(database, "mp", -1)
    own = ring(project([database], head_weight, value_weight), 2)
    own[3:5], from_left, from_right = lax.optimization_barrier((own[3:5], from_left, from_right))
    half = rows // 2
    far_a = hop(from_left[:, :half], "mp", 1)
    far_b = hop(from_right[:, half:], "mp", -1)
    own = ring(own, 3)
    sides = project([from_left, from_right], head_weight, value_weight)
    sides, own[5:7], far_a, far_b = lax.optimization_barrier((sides, own[5:7], far_a, far_b))
    sides = ring(sides, 1)
    far = [[project([far_a, far_b], head_weight, value_weight)]]
    sides[1:3], far = lax.optimization_barrier((sides[1:3], far))
    sides, far = ring(sides, 2), ring(far, 1)
    wanted = after((owner_shard * entries + entry_slot).reshape(-1), sides[1:3])
    plane_wanted = lax.all_gather(wanted, ("y", "c"), axis=0, tiled=False)
    sides[3:5], far[1:3], plane_wanted = lax.optimization_barrier((sides[3:5], far[1:3], plane_wanted))
    sides, far = ring(sides, 3), ring(far, 2)
    sides[5:7], far[3:5] = lax.optimization_barrier((sides[5:7], far[3:5]))

    deltas = jnp.array(DELTAS, jnp.int32)
    shards = (y * NZ + (z + deltas) % NZ) * NC + c
    match = (plane_wanted // entries)[None] == shards[:, None, None]
    asks = jnp.arange(wanted.shape[0], dtype=jnp.int32)
    used = jnp.any(match, axis=2).astype(jnp.int32).reshape(-1)
    seg_at = jnp.sum(jnp.where(match, asks // 2, 0), axis=2).reshape(-1)
    entry_at = jnp.sum(jnp.where(match, (plane_wanted % entries)[None], 0), axis=2).reshape(-1)
    tables = (seg_at, entry_at, used)

    def served(number):
        return attend(CHUNKS[number], tables, qkv, [sum(p, []) for p in zip(own, sides, far)])

    def back(share):
        return lax.all_to_all(share, ("y", "c"), split_axis=0, concat_axis=0, tiled=True)

    first = served(0)
    own[5:7] = after(own[5:7], (sides[5:7], far[3:5]))
    own, sides, far = ring(own), ring(sides, 4), ring(far, 3)
    backs = [back(first)]
    tables = after(tables, first)
    second = served(1)
    own[7], sides[7], far[5:7], second = lax.optimization_barrier((own[7], sides[7], far[5:7], second))
    far = ring(far, 4)
    backs.append(back(after(second, backs[0])))
    tables = after(tables, backs[0])
    backs.append(back(after(served(2), (backs[1], far[7]))))
    backs.append(back(after(served(3), backs[2])))

    owner = owner_shard.reshape(-1)
    delta = (owner // NC % NZ - z) % NZ
    slot = jnp.where(delta < NZ // 2, 2 * delta, 2 * (NZ - delta) - 1)
    src = owner // (NC * NZ) * NC + owner % NC
    return combine(backs, src, slot)


def solution(mesh):
    grid = Mesh(mesh.devices.reshape(NY, NZ, NC, -1), ("y", "z", "c", "mp"))
    group = ("y", "z", "c")
    in_specs = (
        P(group, "mp", None),
        P(None, "mp"),
        P(None, "mp"),
        P(group, "mp"),
        P(group, "mp"),
        P(group, "mp"),
        P(group, None),
        P(group, None),
    )
    return jax.shard_map(
        per_device, mesh=grid, in_specs=in_specs, out_specs=P(group, "mp"), check_vma=False
    )
```

```python
import functools

import jax
import jax.numpy as jnp
from jax import lax
from jax.experimental import pallas as pl
from jax.experimental.pallas import tpu as pltpu
from jax.sharding import Mesh
from jax.sharding import PartitionSpec as P

HEAD_DIM = 128
NY, NZ, NC = 4, 8, 2
PLANE = NY * NC
DELTAS = (0, 7, 1, 6, 2, 5, 3, 4)
CHUNKS = ((0, 1, 2), (3, 4), (5, 6, 7))
STAT = 128
LANES = 16
PAIR = 2


def project_kernel(parts, hw, vw, out, *scratch):
    rows_in, hbuf, vbuf, acc, in_sem, sem = (scratch[:-5], *scratch[-5:])
    entries, _, width = out.shape
    width //= 2
    steps, depth, _ = hbuf.shape
    loads = [pltpu.make_async_copy(p, r, in_sem.at[i]) for i, (p, r) in enumerate(zip(parts, rows_in))]
    weights = [
        [
            pltpu.make_async_copy(w.at[pl.ds(k * depth, depth)], buf.at[k], sem.at[i, k])
            for i, (w, buf) in enumerate(((hw, hbuf), (vw, vbuf)))
        ]
        for k in range(steps)
    ]
    for copy in loads:
        copy.start()
    for pair in weights:
        for copy in pair:
            copy.start()
    for copy in loads:
        copy.wait()
    for k in range(steps):
        for copy in weights[k]:
            copy.wait()
        row = 0
        for r in rows_in:
            count = entries * r.shape[1]
            x = r[:, :, k * depth : (k + 1) * depth].reshape(count, depth)
            for side, buf in ((0, hbuf), (1, vbuf)):
                span = (slice(row, row + count), slice(side * width, (side + 1) * width))
                y = jnp.dot(x, buf[k], preferred_element_type=jnp.float32)
                acc[span] = y if k == 0 else acc[span] + y
            row += count
    row = at = 0
    for r in rows_in:
        rows = r.shape[1]
        block = acc[row : row + entries * rows, :].astype(out.dtype)
        out[:, at : at + rows, :] = block.reshape(entries, rows, 2 * width)
        row += entries * rows
        at += rows


def project(parts, head_weight, value_weight):
    entries, _, depth = parts[0].shape
    rows = sum(p.shape[1] for p in parts)
    width = head_weight.shape[1]
    steps = 8
    n = len(parts)

    def kernel(*refs):
        project_kernel(refs[:n], *refs[n:])

    chunk = pltpu.VMEM((steps, depth // steps, width), jnp.bfloat16)
    return pl.pallas_call(
        kernel,
        in_specs=[pl.BlockSpec(memory_space=pl.ANY)] * (n + 2),
        out_specs=pl.BlockSpec(memory_space=pltpu.VMEM),
        out_shape=jax.ShapeDtypeStruct((entries, rows, 2 * width), jnp.bfloat16),
        scratch_shapes=[pltpu.VMEM(p.shape, p.dtype) for p in parts]
        + [
            chunk,
            chunk,
            pltpu.VMEM((entries * rows, 2 * width), jnp.float32),
            pltpu.SemaphoreType.DMA((n,)),
            pltpu.SemaphoreType.DMA((2, steps)),
        ],
        compiler_params=pltpu.CompilerParams(vmem_limit_bytes=60 << 20),
        cost_estimate=pl.CostEstimate(
            flops=4 * entries * rows * depth * width,
            bytes_accessed=4 * depth * width + 2 * entries * rows * (depth + 2 * width),
            transcendentals=0,
        ),
        name="project",
    )(*parts, head_weight, value_weight)


def matmul(a, b, da, db):
    return lax.dot_general(
        a, b, (((da,), (db,)), ((), ())), preferred_element_type=jnp.float32
    )


def attend_kernel(slots, counts, seg_at, entry_at, used_at, *refs):
    refs = list(refs)
    out = refs.pop()
    qkvs = [[refs.pop(0) for _ in range(PAIR)] for _ in slots]
    held = [[[refs.pop(0) for _ in range(PAIR)] for _ in range(n)] for n in counts]
    seg_len, width = out.shape[1], qkvs[0][0].shape[2] // 3
    factor = HEAD_DIM**-0.5
    lanes = lax.broadcasted_iota(jnp.int32, (seg_len, STAT), 1)
    units = [(s, h) for s in range(PAIR) for h in range(width // HEAD_DIM)]

    def part(ref, index, h):
        begin = index * width + h * HEAD_DIM
        return ref[0, :, begin : begin + HEAD_DIM]

    def run(place, qkv, pieces):
        def rows_of(s, index, h):
            return jnp.concatenate([part(p[s], index, h) for p in pieces], axis=0)

        states = [rows_of(s, 0, h) for s, h in units]
        scores = [
            matmul(part(qkv[s], 1, h), x, 1, 1) * factor for (s, h), x in zip(units, states)
        ]
        peaks = [jnp.max(x, axis=0, keepdims=True) for x in scores]
        scores = [jnp.exp(x - m) for x, m in zip(scores, peaks)]
        weights = [
            (x * (1.0 / jnp.sum(x, axis=0, keepdims=True))).astype(jnp.bfloat16) for x in scores
        ]
        encoded = [
            (x.astype(jnp.float32) + matmul(w, part(qkv[s], 2, h), 0, 0)).astype(jnp.bfloat16)
            for (s, h), x, w in zip(units, states, weights)
        ]
        cross = [
            matmul(part(qkv[s], 0, h), x, 1, 1) * factor for (s, h), x in zip(units, encoded)
        ]
        highest = [jnp.max(x, axis=1, keepdims=True) for x in cross]
        mix = [jnp.exp(x - m) for x, m in zip(cross, highest)]
        totals = [jnp.sum(x, axis=1, keepdims=True) for x in mix]
        shares = []
        for (s, h), x in zip(units, mix):
            upper = x.astype(jnp.bfloat16)
            lower = (x - upper.astype(jnp.float32)).astype(jnp.bfloat16)
            both = matmul(jnp.concatenate([upper, lower], axis=0), rows_of(s, 1, h), 1, 0)
            shares.append(both[:seg_len] + both[seg_len:])
        stats = [out[s, :, len(slots) * width :].astype(jnp.float32) for s in range(PAIR)]
        for (s, h), share, total, high in zip(units, shares, totals, highest):
            begin = place * width + h * HEAD_DIM
            out[s, :, begin : begin + HEAD_DIM] = (share * (1.0 / total)).astype(out.dtype)
            rest = high + jnp.log(total)
            for j in range(3):
                term = rest.astype(jnp.bfloat16).astype(jnp.float32)
                stats[s] = jnp.where(lanes == place * LANES + 3 * h + j, term, stats[s])
                rest = rest - term
        for s in range(PAIR):
            out[s, :, len(slots) * width :] = stats[s].astype(out.dtype)

    for place, (slot, qkv, pieces) in enumerate(zip(slots, qkvs, held)):
        at = slot * PLANE + pl.program_id(0) * PAIR
        used = used_at[at]
        for s in range(1, PAIR):
            used = used | used_at[at + s]
        pl.when(used != 0)(functools.partial(run, place, qkv, pieces))


def attend(slots, tables, qkv, held):
    segs, seg_len, width = qkv.shape
    width //= 3
    seg_dev = segs // PLANE

    def seg_spec(slot, s):
        def index(i, seg, entry, used):
            g = i * PAIR + s
            return g * seg_dev + seg[slot * PLANE + g], 0, 0

        return pl.BlockSpec((1, seg_len, 3 * width), index)

    def piece_spec(piece, slot, s):
        return pl.BlockSpec(
            (1,) + piece.shape[1:],
            lambda i, seg, entry, used: (entry[slot * PLANE + i * PAIR + s], 0, 0),
        )

    in_specs = [seg_spec(slot, s) for slot in slots for s in range(PAIR)]
    args = [*tables] + [qkv] * len(in_specs)
    for slot in slots:
        for piece in held[slot]:
            in_specs += [piece_spec(piece, slot, s) for s in range(PAIR)]
            args += [piece] * PAIR
    full = len(slots) * width + STAT
    return pl.pallas_call(
        functools.partial(attend_kernel, slots, [len(held[slot]) for slot in slots]),
        grid_spec=pltpu.PrefetchScalarGridSpec(
            num_scalar_prefetch=3,
            grid=(PLANE // PAIR,),
            in_specs=in_specs,
            out_specs=pl.BlockSpec((PAIR, seg_len, full), lambda i, *_: (i, 0, 0)),
        ),
        out_shape=jax.ShapeDtypeStruct((PLANE, seg_len, full), jnp.bfloat16),
        compiler_params=pltpu.CompilerParams(vmem_limit_bytes=60 << 20),
        cost_estimate=pl.CostEstimate(flops=len(slots) * (4 << 30), bytes_accessed=1 << 20, transcendentals=0),
        name="attend",
    )(*args)


def combine_kernel(src, slot, *refs):
    backs, out = refs[:-1], refs[-1]
    seg_len = backs[0].shape[1]
    width = out.shape[1]

    def part(i, begin, size, per_place):
        value = None
        for slots, back in zip(CHUNKS, backs):
            here = (slot[i] >= slots[0]) & (slot[i] <= slots[-1])
            offset = jnp.where(here, slot[i] - slots[0], 0) * per_place + begin(len(slots))
            block = back[src[i], :, pl.ds(pl.multiple_of(offset, 128), size)]
            value = block if value is None else jnp.where(here, block, value)
        return value.astype(jnp.float32)

    def total(i):
        first = 0
        for slots in CHUNKS:
            here = (slot[i] >= slots[0]) & (slot[i] <= slots[-1])
            first = jnp.where(here, (slot[i] - slots[0]) * LANES, first)
        x = part(i, lambda n: n * width, STAT, 0)
        x = pltpu.roll(x, STAT - first, 1)
        return x + pltpu.roll(x, STAT - 1, 1) + pltpu.roll(x, STAT - 2, 1)

    @pl.loop(0, out.shape[0] // seg_len, unroll=True)
    def _(s):
        more = total(2 * s + 1) - total(2 * s)
        one = 1.0 / (1.0 + jnp.exp(more))
        two = 1.0 / (1.0 + jnp.exp(-more))
        rows = pl.ds(pl.multiple_of(s * seg_len, seg_len), seg_len)
        for h in range(width // HEAD_DIM):
            first = part(2 * s, lambda n: h * HEAD_DIM, HEAD_DIM, width)
            second = part(2 * s + 1, lambda n: h * HEAD_DIM, HEAD_DIM, width)
            lane = slice(3 * h, 3 * h + 1)
            out[rows, h * HEAD_DIM : (h + 1) * HEAD_DIM] = (
                first * one[:, lane] + second * two[:, lane]
            ).astype(out.dtype)


def combine(backs, src, slot):
    _, seg_len, full = backs[0].shape
    width = (full - STAT) // len(CHUNKS[0])
    return pl.pallas_call(
        combine_kernel,
        in_specs=[pl.BlockSpec(memory_space=pltpu.SMEM)] * 2
        + [pl.BlockSpec(memory_space=pltpu.VMEM)] * len(backs),
        out_specs=pl.BlockSpec(memory_space=pltpu.VMEM),
        out_shape=jax.ShapeDtypeStruct((src.shape[0] // 2 * seg_len, width), jnp.bfloat16),
        compiler_params=pltpu.CompilerParams(vmem_limit_bytes=60 << 20),
        name="combine",
    )(src, slot, *backs)


def hop(x, axis, step):
    n = lax.axis_size(axis)
    return lax.ppermute(x, axis, [(i, (i + step) % n) for i in range(n)])


def after(value, event):
    return lax.optimization_barrier((value, event))[0]


def ring(pieces, hops=NZ // 2, onward=False):
    held = pieces if isinstance(pieces, list) else [[pieces]]
    while len(held) < min(2 * hops + 1, NZ):
        forward, backward = held[-2:] if len(held) > 1 else held * 2
        if len(held) < NZ - 1:
            held = held + [[hop(forward[0], "z", 1)], [hop(backward[0], "z", -1)]]
        else:
            held = held + [[hop(forward[0], "z", 1) if onward else hop(backward[0], "z", -1)]]
    return held


def per_device(
    database,
    head_weight,
    value_weight,
    segment_query,
    segment_key,
    segment_value,
    owner_shard,
    entry_slot,
):
    entries, rows, _ = database.shape
    seg_dev = owner_shard.shape[0]
    seg_len = segment_query.shape[0] // seg_dev
    width = segment_query.shape[1]
    y, z, c = lax.axis_index("y"), lax.axis_index("z"), lax.axis_index("c")

    qkv = jnp.concatenate([segment_query, segment_key, segment_value], axis=1)
    qkv = lax.all_gather(qkv, ("y", "c"), axis=0, tiled=True).reshape(-1, seg_len, 3 * width)

    from_left, from_right = hop(database, "mp", 1), hop(database, "mp", -1)
    own = ring(project([database], head_weight, value_weight), 2)
    own[3:5], from_left, from_right = lax.optimization_barrier((own[3:5], from_left, from_right))
    half = rows // 2
    far_a = hop(from_left[:, :half], "mp", 1)
    far_b = hop(from_right[:, half:], "mp", -1)
    own = ring(own, 3)
    sides = project([from_left, from_right], head_weight, value_weight)
    sides, own[5:7], far_a, far_b = lax.optimization_barrier((sides, own[5:7], far_a, far_b))
    sides = ring(sides, 1)
    far = [[project([far_a, far_b], head_weight, value_weight)]]
    sides[1:3], far = lax.optimization_barrier((sides[1:3], far))
    sides, far = ring(sides, 2), ring(far, 1)
    wanted = after((owner_shard * entries + entry_slot).reshape(-1), sides[1:3])
    plane_wanted = lax.all_gather(wanted, ("y", "c"), axis=0, tiled=False)
    sides[3:5], far[1:3], plane_wanted = lax.optimization_barrier((sides[3:5], far[1:3], plane_wanted))
    sides, far = ring(sides, 3), ring(far, 2)
    sides[5:7], far[3:5] = lax.optimization_barrier((sides[5:7], far[3:5]))

    deltas = jnp.array(DELTAS, jnp.int32)
    shards = (y * NZ + (z + deltas) % NZ) * NC + c
    match = (plane_wanted // entries)[None] == shards[:, None, None]
    asks = jnp.arange(wanted.shape[0], dtype=jnp.int32)
    used = jnp.any(match, axis=2).astype(jnp.int32).reshape(-1)
    seg_at = jnp.sum(jnp.where(match, asks // 2, 0), axis=2).reshape(-1)
    entry_at = jnp.sum(jnp.where(match, (plane_wanted % entries)[None], 0), axis=2).reshape(-1)
    tables = (seg_at, entry_at, used)

    def served(number):
        return attend(CHUNKS[number], tables, qkv, [sum(p, []) for p in zip(own, sides, far)])

    def back(share):
        return lax.all_to_all(share, ("y", "c"), split_axis=0, concat_axis=0, tiled=True)

    first = served(0)
    own[5:7] = after(own[5:7], (sides[5:7], far[3:5]))
    own, sides, far = ring(own), ring(sides, 4, onward=True), ring(far, 3)
    backs = [back(first)]
    tables = after(tables, first)
    second = served(1)
    far[5:7], second = lax.optimization_barrier((far[5:7], second))
    far = ring(far)
    backs.append(back(after(second, backs[0])))
    backs.append(back(after(served(2), backs[1])))

    owner = owner_shard.reshape(-1)
    delta = (owner // NC % NZ - z) % NZ
    slot = jnp.where(delta < NZ // 2, 2 * delta, 2 * (NZ - delta) - 1)
    src = owner // (NC * NZ) * NC + owner % NC
    return combine(backs, src, slot)


def solution(mesh):
    grid = Mesh(mesh.devices.reshape(NY, NZ, NC, -1), ("y", "z", "c", "mp"))
    group = ("y", "z", "c")
    in_specs = (
        P(group, "mp", None),
        P(None, "mp"),
        P(None, "mp"),
        P(group, "mp"),
        P(group, "mp"),
        P(group, "mp"),
        P(group, None),
        P(group, None),
    )
    return jax.shard_map(
        per_device, mesh=grid, in_specs=in_specs, out_specs=P(group, "mp"), check_vma=False
    )
```

```python
import functools

import jax
import jax.numpy as jnp
from jax import lax
from jax.experimental import pallas as pl
from jax.experimental.pallas import tpu as pltpu
from jax.sharding import Mesh
from jax.sharding import PartitionSpec as P

HEAD_DIM = 128
NY, NZ, NC = 4, 8, 2
PLANE = NY * NC
DELTAS = (0, 7, 1, 6, 2, 5, 3, 4)
CHUNKS = ((0, 1, 2), (3, 4), (5, 6, 7))
STAT = 128
LANES = 16
PAIR = 2


def project_kernel(parts, hw, vw, out, *scratch):
    rows_in, hbuf, vbuf, acc, in_sem, sem = (scratch[:-5], *scratch[-5:])
    entries, _, width = out.shape
    width //= 2
    steps, depth, _ = hbuf.shape
    loads = [pltpu.make_async_copy(p, r, in_sem.at[i]) for i, (p, r) in enumerate(zip(parts, rows_in))]
    weights = [
        [
            pltpu.make_async_copy(w.at[pl.ds(k * depth, depth)], buf.at[k], sem.at[i, k])
            for i, (w, buf) in enumerate(((hw, hbuf), (vw, vbuf)))
        ]
        for k in range(steps)
    ]
    for copy in loads:
        copy.start()
    for pair in weights:
        for copy in pair:
            copy.start()
    for copy in loads:
        copy.wait()
    for k in range(steps):
        for copy in weights[k]:
            copy.wait()
        row = 0
        for r in rows_in:
            count = entries * r.shape[1]
            x = r[:, :, k * depth : (k + 1) * depth].reshape(count, depth)
            for side, buf in ((0, hbuf), (1, vbuf)):
                span = (slice(row, row + count), slice(side * width, (side + 1) * width))
                y = jnp.dot(x, buf[k], preferred_element_type=jnp.float32)
                acc[span] = y if k == 0 else acc[span] + y
            row += count
    row = at = 0
    for r in rows_in:
        rows = r.shape[1]
        block = acc[row : row + entries * rows, :].astype(out.dtype)
        out[:, at : at + rows, :] = block.reshape(entries, rows, 2 * width)
        row += entries * rows
        at += rows


def project(parts, head_weight, value_weight):
    entries, _, depth = parts[0].shape
    rows = sum(p.shape[1] for p in parts)
    width = head_weight.shape[1]
    steps = 8
    n = len(parts)

    def kernel(*refs):
        project_kernel(refs[:n], *refs[n:])

    chunk = pltpu.VMEM((steps, depth // steps, width), jnp.bfloat16)
    return pl.pallas_call(
        kernel,
        in_specs=[pl.BlockSpec(memory_space=pl.ANY)] * (n + 2),
        out_specs=pl.BlockSpec(memory_space=pltpu.VMEM),
        out_shape=jax.ShapeDtypeStruct((entries, rows, 2 * width), jnp.bfloat16),
        scratch_shapes=[pltpu.VMEM(p.shape, p.dtype) for p in parts]
        + [
            chunk,
            chunk,
            pltpu.VMEM((entries * rows, 2 * width), jnp.float32),
            pltpu.SemaphoreType.DMA((n,)),
            pltpu.SemaphoreType.DMA((2, steps)),
        ],
        compiler_params=pltpu.CompilerParams(vmem_limit_bytes=60 << 20),
        cost_estimate=pl.CostEstimate(
            flops=4 * entries * rows * depth * width,
            bytes_accessed=4 * depth * width + 2 * entries * rows * (depth + 2 * width),
            transcendentals=0,
        ),
        name="project",
    )(*parts, head_weight, value_weight)


def matmul(a, b, da, db):
    return lax.dot_general(
        a, b, (((da,), (db,)), ((), ())), preferred_element_type=jnp.float32
    )


def attend_kernel(slots, chunk, chained, counts, seg_at, entry_at, used_at, *refs):
    refs = list(refs)
    out = refs.pop()
    if chained:
        out[...] = refs.pop()[...]
    qkvs = [[refs.pop(0) for _ in range(PAIR)] for _ in slots]
    held = [[[refs.pop(0) for _ in range(PAIR)] for _ in range(n)] for n in counts]
    seg_len, width = out.shape[1], qkvs[0][0].shape[2] // 3
    factor = HEAD_DIM**-0.5
    lanes = lax.broadcasted_iota(jnp.int32, (seg_len, STAT), 1)
    units = [(s, h) for s in range(PAIR) for h in range(width // HEAD_DIM)]

    def part(ref, index, h):
        begin = index * width + h * HEAD_DIM
        return ref[0, :, begin : begin + HEAD_DIM]

    def run(place, qkv, pieces):
        def rows_of(s, index, h):
            return jnp.concatenate([part(p[s], index, h) for p in pieces], axis=0)

        states = [rows_of(s, 0, h) for s, h in units]
        scores = [
            matmul(part(qkv[s], 1, h), x, 1, 1) * factor for (s, h), x in zip(units, states)
        ]
        peaks = [jnp.max(x, axis=0, keepdims=True) for x in scores]
        scores = [jnp.exp(x - m) for x, m in zip(scores, peaks)]
        weights = [
            (x * (1.0 / jnp.sum(x, axis=0, keepdims=True))).astype(jnp.bfloat16) for x in scores
        ]
        encoded = [
            (x.astype(jnp.float32) + matmul(w, part(qkv[s], 2, h), 0, 0)).astype(jnp.bfloat16)
            for (s, h), x, w in zip(units, states, weights)
        ]
        cross = [
            matmul(part(qkv[s], 0, h), x, 1, 1) * factor for (s, h), x in zip(units, encoded)
        ]
        highest = [jnp.max(x, axis=1, keepdims=True) for x in cross]
        mix = [jnp.exp(x - m) for x, m in zip(cross, highest)]
        totals = [jnp.sum(x, axis=1, keepdims=True) for x in mix]
        shares = []
        for (s, h), x in zip(units, mix):
            upper = x.astype(jnp.bfloat16)
            lower = (x - upper.astype(jnp.float32)).astype(jnp.bfloat16)
            both = matmul(jnp.concatenate([upper, lower], axis=0), rows_of(s, 1, h), 1, 0)
            shares.append(both[:seg_len] + both[seg_len:])
        stats = [out[s, :, len(chunk) * width :].astype(jnp.float32) for s in range(PAIR)]
        for (s, h), share, total, high in zip(units, shares, totals, highest):
            begin = place * width + h * HEAD_DIM
            out[s, :, begin : begin + HEAD_DIM] = (share * (1.0 / total)).astype(out.dtype)
            rest = high + jnp.log(total)
            for j in range(3):
                term = rest.astype(jnp.bfloat16).astype(jnp.float32)
                stats[s] = jnp.where(lanes == place * LANES + 3 * h + j, term, stats[s])
                rest = rest - term
        for s in range(PAIR):
            out[s, :, len(chunk) * width :] = stats[s].astype(out.dtype)

    for slot, qkv, pieces in zip(slots, qkvs, held):
        at = slot * PLANE + pl.program_id(0) * PAIR
        used = used_at[at]
        for s in range(1, PAIR):
            used = used | used_at[at + s]
        pl.when(used != 0)(functools.partial(run, chunk.index(slot), qkv, pieces))


def attend(slots, chunk, tables, qkv, held, previous=None):
    segs, seg_len, width = qkv.shape
    width //= 3
    seg_dev = segs // PLANE

    def seg_spec(slot, s):
        def index(i, seg, entry, used):
            g = i * PAIR + s
            return g * seg_dev + seg[slot * PLANE + g], 0, 0

        return pl.BlockSpec((1, seg_len, 3 * width), index)

    def piece_spec(piece, slot, s):
        return pl.BlockSpec(
            (1,) + piece.shape[1:],
            lambda i, seg, entry, used: (entry[slot * PLANE + i * PAIR + s], 0, 0),
        )

    in_specs = [seg_spec(slot, s) for slot in slots for s in range(PAIR)]
    args = [*tables] + [qkv] * len(in_specs)
    for slot in slots:
        for piece in held[slot]:
            in_specs += [piece_spec(piece, slot, s) for s in range(PAIR)]
            args += [piece] * PAIR
    full = len(chunk) * width + STAT
    if previous is not None:
        in_specs.append(pl.BlockSpec((PAIR, seg_len, full), lambda i, *_: (i, 0, 0)))
        args.append(previous)
    return pl.pallas_call(
        functools.partial(attend_kernel, slots, chunk, previous is not None, [len(held[slot]) for slot in slots]),
        grid_spec=pltpu.PrefetchScalarGridSpec(
            num_scalar_prefetch=3,
            grid=(PLANE // PAIR,),
            in_specs=in_specs,
            out_specs=pl.BlockSpec((PAIR, seg_len, full), lambda i, *_: (i, 0, 0)),
        ),
        out_shape=jax.ShapeDtypeStruct((PLANE, seg_len, full), jnp.bfloat16),
        compiler_params=pltpu.CompilerParams(vmem_limit_bytes=60 << 20),
        cost_estimate=pl.CostEstimate(flops=len(slots) * (6 << 30), bytes_accessed=1 << 20, transcendentals=0),
        name="attend",
    )(*args)


def combine_kernel(src, slot, *refs):
    backs, out = refs[:-1], refs[-1]
    seg_len = backs[0].shape[1]
    width = out.shape[1]

    def part(i, begin, size, per_place):
        value = None
        for slots, back in zip(CHUNKS, backs):
            here = (slot[i] >= slots[0]) & (slot[i] <= slots[-1])
            offset = jnp.where(here, slot[i] - slots[0], 0) * per_place + begin(len(slots))
            block = back[src[i], :, pl.ds(pl.multiple_of(offset, 128), size)]
            value = block if value is None else jnp.where(here, block, value)
        return value.astype(jnp.float32)

    def total(i):
        first = 0
        for slots in CHUNKS:
            here = (slot[i] >= slots[0]) & (slot[i] <= slots[-1])
            first = jnp.where(here, (slot[i] - slots[0]) * LANES, first)
        x = part(i, lambda n: n * width, STAT, 0)
        x = pltpu.roll(x, STAT - first, 1)
        return x + pltpu.roll(x, STAT - 1, 1) + pltpu.roll(x, STAT - 2, 1)

    @pl.loop(0, out.shape[0] // seg_len, unroll=True)
    def _(s):
        more = total(2 * s + 1) - total(2 * s)
        one = 1.0 / (1.0 + jnp.exp(more))
        two = 1.0 / (1.0 + jnp.exp(-more))
        rows = pl.ds(pl.multiple_of(s * seg_len, seg_len), seg_len)
        for h in range(width // HEAD_DIM):
            first = part(2 * s, lambda n: h * HEAD_DIM, HEAD_DIM, width)
            second = part(2 * s + 1, lambda n: h * HEAD_DIM, HEAD_DIM, width)
            lane = slice(3 * h, 3 * h + 1)
            out[rows, h * HEAD_DIM : (h + 1) * HEAD_DIM] = (
                first * one[:, lane] + second * two[:, lane]
            ).astype(out.dtype)


def combine(backs, src, slot):
    _, seg_len, full = backs[0].shape
    width = (full - STAT) // len(CHUNKS[0])
    return pl.pallas_call(
        combine_kernel,
        in_specs=[pl.BlockSpec(memory_space=pltpu.SMEM)] * 2
        + [pl.BlockSpec(memory_space=pltpu.VMEM)] * len(backs),
        out_specs=pl.BlockSpec(memory_space=pltpu.VMEM),
        out_shape=jax.ShapeDtypeStruct((src.shape[0] // 2 * seg_len, width), jnp.bfloat16),
        compiler_params=pltpu.CompilerParams(vmem_limit_bytes=24 << 20),
        name="combine",
    )(src, slot, *backs)


def hop(x, axis, step):
    n = lax.axis_size(axis)
    return lax.ppermute(x, axis, [(i, (i + step) % n) for i in range(n)])


def after(value, event):
    return lax.optimization_barrier((value, event))[0]


def ring(pieces, hops=NZ // 2, onward=False):
    held = pieces if isinstance(pieces, list) else [[pieces]]
    while len(held) < min(2 * hops + 1, NZ):
        forward, backward = held[-2:] if len(held) > 1 else held * 2
        if len(held) < NZ - 1:
            held = held + [[hop(forward[0], "z", 1)], [hop(backward[0], "z", -1)]]
        else:
            held = held + [[hop(forward[0], "z", 1) if onward else hop(backward[0], "z", -1)]]
    return held


def per_device(
    database,
    head_weight,
    value_weight,
    segment_query,
    segment_key,
    segment_value,
    owner_shard,
    entry_slot,
):
    entries, rows, _ = database.shape
    seg_dev = owner_shard.shape[0]
    seg_len = segment_query.shape[0] // seg_dev
    width = segment_query.shape[1]
    y, z, c = lax.axis_index("y"), lax.axis_index("z"), lax.axis_index("c")

    qkv = jnp.concatenate([segment_query, segment_key, segment_value], axis=1)
    qkv = lax.all_gather(qkv, ("y", "c"), axis=0, tiled=True).reshape(-1, seg_len, 3 * width)

    from_left, from_right = hop(database, "mp", 1), hop(database, "mp", -1)
    own = ring(project([database], head_weight, value_weight), 2)
    own[3:5], from_left, from_right = lax.optimization_barrier((own[3:5], from_left, from_right))
    half = rows // 2
    far_a = hop(from_left[:, :half], "mp", 1)
    far_b = hop(from_right[:, half:], "mp", -1)
    own = ring(own, 3)
    sides = project([from_left, from_right], head_weight, value_weight)
    sides, own[5:7], far_a, far_b = lax.optimization_barrier((sides, own[5:7], far_a, far_b))
    sides = ring(sides, 1)
    far = [[project([far_a, far_b], head_weight, value_weight)]]
    sides[1:3], far = lax.optimization_barrier((sides[1:3], far))
    sides, far = ring(sides, 2), ring(far, 1)
    wanted = after((owner_shard * entries + entry_slot).reshape(-1), sides[1:3])
    plane_wanted = lax.all_gather(wanted, ("y", "c"), axis=0, tiled=False)
    sides[3:5], far[1:3], plane_wanted = lax.optimization_barrier((sides[3:5], far[1:3], plane_wanted))
    sides, far = ring(sides, 3), ring(far, 2)
    sides[5:7], far[3:5] = lax.optimization_barrier((sides[5:7], far[3:5]))

    deltas = jnp.array(DELTAS, jnp.int32)
    shards = (y * NZ + (z + deltas) % NZ) * NC + c
    match = (plane_wanted // entries)[None] == shards[:, None, None]
    asks = jnp.arange(wanted.shape[0], dtype=jnp.int32)
    used = jnp.any(match, axis=2).astype(jnp.int32).reshape(-1)
    seg_at = jnp.sum(jnp.where(match, asks // 2, 0), axis=2).reshape(-1)
    entry_at = jnp.sum(jnp.where(match, (plane_wanted % entries)[None], 0), axis=2).reshape(-1)
    tables = (seg_at, entry_at, used)

    def served(number, slots, previous=None):
        held = [sum(p, []) for p in zip(own, sides, far)]
        return attend(slots, CHUNKS[number], tables, qkv, held, previous)

    def back(share):
        return lax.all_to_all(share, ("y", "c"), split_axis=0, concat_axis=0, tiled=True)

    first = served(0, CHUNKS[0])
    own[5:7] = after(own[5:7], (sides[5:7], far[3:5]))
    own, sides, far = ring(own), ring(sides, 4, onward=True), ring(far, 3)
    backs = [back(first)]
    tables = after(tables, first)
    second = served(1, CHUNKS[1])
    far[5:7], second = lax.optimization_barrier((far[5:7], second))
    far = ring(far)
    backs.append(back(after(second, backs[0])))
    third = served(2, CHUNKS[2][:2])
    third = served(2, CHUNKS[2][2:], third)
    backs.append(back(after(third, backs[1])))

    owner = owner_shard.reshape(-1)
    delta = (owner // NC % NZ - z) % NZ
    slot = jnp.where(delta < NZ // 2, 2 * delta, 2 * (NZ - delta) - 1)
    src = owner // (NC * NZ) * NC + owner % NC
    return combine(backs, src, slot)


def solution(mesh):
    grid = Mesh(mesh.devices.reshape(NY, NZ, NC, -1), ("y", "z", "c", "mp"))
    group = ("y", "z", "c")
    in_specs = (
        P(group, "mp", None),
        P(None, "mp"),
        P(None, "mp"),
        P(group, "mp"),
        P(group, "mp"),
        P(group, "mp"),
        P(group, None),
        P(group, None),
    )
    return jax.shard_map(
        per_device, mesh=grid, in_specs=in_specs, out_specs=P(group, "mp"), check_vma=False
    )
```

```python
import functools

import jax
import jax.numpy as jnp
from jax import lax
from jax.experimental import pallas as pl
from jax.experimental.pallas import tpu as pltpu
from jax.sharding import Mesh
from jax.sharding import PartitionSpec as P

HEAD_DIM = 128
NY, NZ, NC = 4, 8, 2
PLANE = NY * NC
DELTAS = (0, 7, 1, 6, 2, 5, 3, 4)
CHUNKS = ((0, 1, 2), (3, 4), (5, 6, 7))
STAT = 128
LANES = 16
PAIR = 2


def project_kernel(parts, hw, vw, out, *scratch):
    rows_in, hbuf, vbuf, acc, in_sem, sem = (scratch[:-5], *scratch[-5:])
    entries, _, width = out.shape
    width //= 2
    steps, depth, _ = hbuf.shape
    loads = [pltpu.make_async_copy(p, r, in_sem.at[i]) for i, (p, r) in enumerate(zip(parts, rows_in))]
    weights = [
        [
            pltpu.make_async_copy(w.at[pl.ds(k * depth, depth)], buf.at[k], sem.at[i, k])
            for i, (w, buf) in enumerate(((hw, hbuf), (vw, vbuf)))
        ]
        for k in range(steps)
    ]
    for copy in loads:
        copy.start()
    for pair in weights:
        for copy in pair:
            copy.start()
    for copy in loads:
        copy.wait()
    for k in range(steps):
        for copy in weights[k]:
            copy.wait()
        row = 0
        for r in rows_in:
            count = entries * r.shape[1]
            x = r[:, :, k * depth : (k + 1) * depth].reshape(count, depth)
            for side, buf in ((0, hbuf), (1, vbuf)):
                span = (slice(row, row + count), slice(side * width, (side + 1) * width))
                y = jnp.dot(x, buf[k], preferred_element_type=jnp.float32)
                acc[span] = y if k == 0 else acc[span] + y
            row += count
    row = at = 0
    for r in rows_in:
        rows = r.shape[1]
        block = acc[row : row + entries * rows, :].astype(out.dtype)
        out[:, at : at + rows, :] = block.reshape(entries, rows, 2 * width)
        row += entries * rows
        at += rows


def project(parts, head_weight, value_weight):
    entries, _, depth = parts[0].shape
    rows = sum(p.shape[1] for p in parts)
    width = head_weight.shape[1]
    steps = 4
    n = len(parts)

    def kernel(*refs):
        project_kernel(refs[:n], *refs[n:])

    chunk = pltpu.VMEM((steps, depth // steps, width), jnp.bfloat16)
    return pl.pallas_call(
        kernel,
        in_specs=[pl.BlockSpec(memory_space=pl.ANY)] * (n + 2),
        out_specs=pl.BlockSpec(memory_space=pltpu.VMEM),
        out_shape=jax.ShapeDtypeStruct((entries, rows, 2 * width), jnp.bfloat16),
        scratch_shapes=[pltpu.VMEM(p.shape, p.dtype) for p in parts]
        + [
            chunk,
            chunk,
            pltpu.VMEM((entries * rows, 2 * width), jnp.float32),
            pltpu.SemaphoreType.DMA((n,)),
            pltpu.SemaphoreType.DMA((2, steps)),
        ],
        compiler_params=pltpu.CompilerParams(vmem_limit_bytes=60 << 20),
        cost_estimate=pl.CostEstimate(
            flops=4 * entries * rows * depth * width,
            bytes_accessed=4 * depth * width + 2 * entries * rows * (depth + 2 * width),
            transcendentals=0,
        ),
        name="project",
    )(*parts, head_weight, value_weight)


def matmul(a, b, da, db):
    return lax.dot_general(
        a, b, (((da,), (db,)), ((), ())), preferred_element_type=jnp.float32
    )


def attend_kernel(slots, chunk, chained, counts, seg_at, entry_at, used_at, *refs):
    refs = list(refs)
    out = refs.pop()
    if chained:
        out[...] = refs.pop()[...]
    qkvs = [[refs.pop(0) for _ in range(PAIR)] for _ in slots]
    held = [[[refs.pop(0) for _ in range(PAIR)] for _ in range(n)] for n in counts]
    seg_len, width = out.shape[1], qkvs[0][0].shape[2] // 3
    factor = HEAD_DIM**-0.5
    lanes = lax.broadcasted_iota(jnp.int32, (seg_len, STAT), 1)
    units = [(s, h) for s in range(PAIR) for h in range(width // HEAD_DIM)]

    def part(ref, index, h):
        begin = index * width + h * HEAD_DIM
        return ref[0, :, begin : begin + HEAD_DIM]

    def run(place, qkv, pieces):
        def rows_of(s, index, h):
            return jnp.concatenate([part(p[s], index, h) for p in pieces], axis=0)

        states = [rows_of(s, 0, h) for s, h in units]
        scores = [
            matmul(part(qkv[s], 1, h), x, 1, 1) * factor for (s, h), x in zip(units, states)
        ]
        peaks = [jnp.max(x, axis=0, keepdims=True) for x in scores]
        scores = [jnp.exp(x - m) for x, m in zip(scores, peaks)]
        weights = [
            (x * (1.0 / jnp.sum(x, axis=0, keepdims=True))).astype(jnp.bfloat16) for x in scores
        ]
        encoded = [
            (x.astype(jnp.float32) + matmul(w, part(qkv[s], 2, h), 0, 0)).astype(jnp.bfloat16)
            for (s, h), x, w in zip(units, states, weights)
        ]
        cross = [
            matmul(part(qkv[s], 0, h), x, 1, 1) * factor for (s, h), x in zip(units, encoded)
        ]
        highest = [jnp.max(x, axis=1, keepdims=True) for x in cross]
        mix = [jnp.exp(x - m) for x, m in zip(cross, highest)]
        totals = [jnp.sum(x, axis=1, keepdims=True) for x in mix]
        shares = []
        for (s, h), x in zip(units, mix):
            upper = x.astype(jnp.bfloat16)
            lower = (x - upper.astype(jnp.float32)).astype(jnp.bfloat16)
            both = matmul(jnp.concatenate([upper, lower], axis=0), rows_of(s, 1, h), 1, 0)
            shares.append(both[:seg_len] + both[seg_len:])
        stats = [out[s, :, len(chunk) * width :].astype(jnp.float32) for s in range(PAIR)]
        for (s, h), share, total, high in zip(units, shares, totals, highest):
            begin = place * width + h * HEAD_DIM
            out[s, :, begin : begin + HEAD_DIM] = (share * (1.0 / total)).astype(out.dtype)
            rest = high + jnp.log(total)
            for j in range(3):
                term = rest.astype(jnp.bfloat16).astype(jnp.float32)
                stats[s] = jnp.where(lanes == place * LANES + 3 * h + j, term, stats[s])
                rest = rest - term
        for s in range(PAIR):
            out[s, :, len(chunk) * width :] = stats[s].astype(out.dtype)

    for slot, qkv, pieces in zip(slots, qkvs, held):
        at = slot * PLANE + pl.program_id(0) * PAIR
        used = used_at[at]
        for s in range(1, PAIR):
            used = used | used_at[at + s]
        pl.when(used != 0)(functools.partial(run, chunk.index(slot), qkv, pieces))


def attend(slots, chunk, tables, qkv, held, previous=None):
    segs, seg_len, width = qkv.shape
    width //= 3
    seg_dev = segs // PLANE

    def seg_spec(slot, s):
        def index(i, seg, entry, used):
            g = i * PAIR + s
            return g * seg_dev + seg[slot * PLANE + g], 0, 0

        return pl.BlockSpec((1, seg_len, 3 * width), index)

    def piece_spec(piece, slot, s):
        return pl.BlockSpec(
            (1,) + piece.shape[1:],
            lambda i, seg, entry, used: (entry[slot * PLANE + i * PAIR + s], 0, 0),
        )

    in_specs = [seg_spec(slot, s) for slot in slots for s in range(PAIR)]
    args = [*tables] + [qkv] * len(in_specs)
    for slot in slots:
        for piece in held[slot]:
            in_specs += [piece_spec(piece, slot, s) for s in range(PAIR)]
            args += [piece] * PAIR
    full = len(chunk) * width + STAT
    if previous is not None:
        in_specs.append(pl.BlockSpec((PAIR, seg_len, full), lambda i, *_: (i, 0, 0)))
        args.append(previous)
    return pl.pallas_call(
        functools.partial(attend_kernel, slots, chunk, previous is not None, [len(held[slot]) for slot in slots]),
        grid_spec=pltpu.PrefetchScalarGridSpec(
            num_scalar_prefetch=3,
            grid=(PLANE // PAIR,),
            in_specs=in_specs,
            out_specs=pl.BlockSpec((PAIR, seg_len, full), lambda i, *_: (i, 0, 0)),
        ),
        out_shape=jax.ShapeDtypeStruct((PLANE, seg_len, full), jnp.bfloat16),
        compiler_params=pltpu.CompilerParams(vmem_limit_bytes=60 << 20),
        cost_estimate=pl.CostEstimate(flops=len(slots) * (6 << 30), bytes_accessed=1 << 20, transcendentals=0),
        name="attend",
    )(*args)


def combine_kernel(src, slot, *refs):
    backs, out = refs[:-1], refs[-1]
    seg_len = backs[0].shape[1]
    width = out.shape[1]

    def part(i, begin, size, per_place):
        value = None
        for slots, back in zip(CHUNKS, backs):
            here = (slot[i] >= slots[0]) & (slot[i] <= slots[-1])
            offset = jnp.where(here, slot[i] - slots[0], 0) * per_place + begin(len(slots))
            block = back[src[i], :, pl.ds(pl.multiple_of(offset, 128), size)]
            value = block if value is None else jnp.where(here, block, value)
        return value.astype(jnp.float32)

    def total(i):
        first = 0
        for slots in CHUNKS:
            here = (slot[i] >= slots[0]) & (slot[i] <= slots[-1])
            first = jnp.where(here, (slot[i] - slots[0]) * LANES, first)
        x = part(i, lambda n: n * width, STAT, 0)
        x = pltpu.roll(x, STAT - first, 1)
        return x + pltpu.roll(x, STAT - 1, 1) + pltpu.roll(x, STAT - 2, 1)

    @pl.loop(0, out.shape[0] // seg_len, unroll=True)
    def _(s):
        more = total(2 * s + 1) - total(2 * s)
        one = 1.0 / (1.0 + jnp.exp(more))
        two = 1.0 / (1.0 + jnp.exp(-more))
        rows = pl.ds(pl.multiple_of(s * seg_len, seg_len), seg_len)
        for h in range(width // HEAD_DIM):
            first = part(2 * s, lambda n: h * HEAD_DIM, HEAD_DIM, width)
            second = part(2 * s + 1, lambda n: h * HEAD_DIM, HEAD_DIM, width)
            lane = slice(3 * h, 3 * h + 1)
            out[rows, h * HEAD_DIM : (h + 1) * HEAD_DIM] = (
                first * one[:, lane] + second * two[:, lane]
            ).astype(out.dtype)


def combine(backs, src, slot):
    _, seg_len, full = backs[0].shape
    width = (full - STAT) // len(CHUNKS[0])
    return pl.pallas_call(
        combine_kernel,
        in_specs=[pl.BlockSpec(memory_space=pltpu.SMEM)] * 2
        + [pl.BlockSpec(memory_space=pltpu.VMEM)] * len(backs),
        out_specs=pl.BlockSpec(memory_space=pltpu.VMEM),
        out_shape=jax.ShapeDtypeStruct((src.shape[0] // 2 * seg_len, width), jnp.bfloat16),
        compiler_params=pltpu.CompilerParams(vmem_limit_bytes=24 << 20),
        name="combine",
    )(src, slot, *backs)


def hop(x, axis, step):
    n = lax.axis_size(axis)
    return lax.ppermute(x, axis, [(i, (i + step) % n) for i in range(n)])


def after(value, event):
    return lax.optimization_barrier((value, event))[0]


def ring(pieces, hops=NZ // 2, onward=False):
    held = pieces if isinstance(pieces, list) else [[pieces]]
    while len(held) < min(2 * hops + 1, NZ):
        forward, backward = held[-2:] if len(held) > 1 else held * 2
        if len(held) < NZ - 1:
            held = held + [[hop(forward[0], "z", 1)], [hop(backward[0], "z", -1)]]
        else:
            held = held + [[hop(forward[0], "z", 1) if onward else hop(backward[0], "z", -1)]]
    return held


def per_device(
    database,
    head_weight,
    value_weight,
    segment_query,
    segment_key,
    segment_value,
    owner_shard,
    entry_slot,
):
    entries, rows, _ = database.shape
    seg_dev = owner_shard.shape[0]
    seg_len = segment_query.shape[0] // seg_dev
    width = segment_query.shape[1]
    y, z, c = lax.axis_index("y"), lax.axis_index("z"), lax.axis_index("c")

    qkv = jnp.concatenate([segment_query, segment_key, segment_value], axis=1)
    qkv = lax.all_gather(qkv, ("y", "c"), axis=0, tiled=True).reshape(-1, seg_len, 3 * width)

    from_left, from_right = hop(database, "mp", 1), hop(database, "mp", -1)
    own = ring(project([database], head_weight, value_weight), 2)
    own[3:5], from_left, from_right = lax.optimization_barrier((own[3:5], from_left, from_right))
    half = rows // 2
    far_a = hop(from_left[:, :half], "mp", 1)
    far_b = hop(from_right[:, half:], "mp", -1)
    own = ring(own, 3)
    sides = project([from_left, from_right], head_weight, value_weight)
    sides, own[5:7], far_a, far_b = lax.optimization_barrier((sides, own[5:7], far_a, far_b))
    sides = ring(sides, 1)
    far = [[project([far_a, far_b], head_weight, value_weight)]]
    sides[1:3], far = lax.optimization_barrier((sides[1:3], far))
    sides, far = ring(sides, 2), ring(far, 1)
    wanted = after((owner_shard * entries + entry_slot).reshape(-1), sides[1:3])
    plane_wanted = lax.all_gather(wanted, ("y", "c"), axis=0, tiled=False)
    sides[3:5], far[1:3], plane_wanted = lax.optimization_barrier((sides[3:5], far[1:3], plane_wanted))
    sides, far = ring(sides, 3), ring(far, 2)
    sides[5:7], far[3:5] = lax.optimization_barrier((sides[5:7], far[3:5]))

    deltas = jnp.array(DELTAS, jnp.int32)
    shards = (y * NZ + (z + deltas) % NZ) * NC + c
    match = (plane_wanted // entries)[None] == shards[:, None, None]
    asks = jnp.arange(wanted.shape[0], dtype=jnp.int32)
    used = jnp.any(match, axis=2).astype(jnp.int32).reshape(-1)
    seg_at = jnp.sum(jnp.where(match, asks // 2, 0), axis=2).reshape(-1)
    entry_at = jnp.sum(jnp.where(match, (plane_wanted % entries)[None], 0), axis=2).reshape(-1)
    tables = (seg_at, entry_at, used)

    def served(number, slots, previous=None):
        held = [sum(p, []) for p in zip(own, sides, far)]
        return attend(slots, CHUNKS[number], tables, qkv, held, previous)

    def back(share):
        return lax.all_to_all(share, ("y", "c"), split_axis=0, concat_axis=0, tiled=True)

    first = served(0, CHUNKS[0])
    own[5:7] = after(own[5:7], (sides[5:7], far[3:5]))
    own, sides, far = ring(own), ring(sides, 4, onward=True), ring(far, 3)
    backs = [back(first)]
    tables = after(tables, first)
    second = served(1, CHUNKS[1])
    far[5:7], second = lax.optimization_barrier((far[5:7], second))
    far = ring(far)
    backs.append(back(after(second, backs[0])))
    third = served(2, CHUNKS[2][:2])
    third = served(2, CHUNKS[2][2:], third)
    backs.append(back(after(third, backs[1])))

    owner = owner_shard.reshape(-1)
    delta = (owner // NC % NZ - z) % NZ
    slot = jnp.where(delta < NZ // 2, 2 * delta, 2 * (NZ - delta) - 1)
    src = owner // (NC * NZ) * NC + owner % NC
    return combine(backs, src, slot)


def solution(mesh):
    grid = Mesh(mesh.devices.reshape(NY, NZ, NC, -1), ("y", "z", "c", "mp"))
    group = ("y", "z", "c")
    in_specs = (
        P(group, "mp", None),
        P(None, "mp"),
        P(None, "mp"),
        P(group, "mp"),
        P(group, "mp"),
        P(group, "mp"),
        P(group, None),
        P(group, None),
    )
    return jax.shard_map(
        per_device, mesh=grid, in_specs=in_specs, out_specs=P(group, "mp"), check_vma=False
    )
```
